32 devices in a mesh: seq: 8 (over z, x), head: 4 (over y, core).
Axes of the slice: x: 2, y: 2, z: 4, core: 2. Of those that a mesh axis runs over, the one named last changes fastest.
Arguments:
- block_input: bfloat16 [1024, 1024], P('seq', 'head'), may hold values from -6 to 6
- mixer_gain: bfloat16 [1024], P('head'), may hold values from 0.5 to 1.5
- proj_weight: bfloat16 [1024, 8, 512], P(None, 'head'), may hold values from -0.1875 to 0.1875
- rate_weight: bfloat16 [1024, 8, 2], P(None, 'head'), may hold values from -0.1875 to 0.1875
- conv_weight: float32 [4, 8, 384], P(None, 'head'), may hold values from -3 to 3
- decay_log: float32 [8], P('head'), may hold values from -13 to -3
- decay_bias: float32 [8], P('head'), may hold values from -2 to 1
- write_bias: float32 [8], P('head'), may hold values from -6 to -2
- output_gain: float32 [8, 128], P('head'), may hold values from 0.5 to 1.5
- merge_weight: bfloat16 [1024, 1024], P('head'), may hold values from -0.375 to 0.375
- feed_gain: bfloat16 [1024], P('head'), may hold values from 0.5 to 1.5
- gateup_weight: bfloat16 [1024, 2, 2816], P(None, None, 'head'), may hold values from -0.1875 to 0.1875
- down_weight: bfloat16 [2816, 1024], P('head'), may hold values from -0.21875 to 0.21875
- output_grad: bfloat16 [1024, 1024], P('seq', 'head'), may hold values from -6 to 6
Outputs:
- block_output: float32 [1024, 1024], P('seq', 'head')
- input_grad: float32 [1024, 1024], P('seq', 'head')
- mixer_gain_grad: float32 [1024], P('head')
- proj_weight_grad: float32 [1024, 8, 512], P('seq', 'head')
- rate_weight_grad: float32 [1024, 8, 2], P('seq', 'head')
- conv_weight_grad: float32 [4, 8, 384], P(None, 'head', 'seq')
- decay_log_grad: float32 [8], P('head')
- decay_bias_grad: float32 [8], P('head')
- write_bias_grad: float32 [8], P('head')
- output_gain_grad: float32 [8, 128], P('head', 'seq')
- merge_weight_grad: float32 [1024, 1024], P('head', 'seq')
- feed_gain_grad: float32 [1024], P('head')
- gateup_weight_grad: float32 [1024, 2, 2816], P('seq', None, 'head')
- down_weight_grad: float32 [2816, 1024], P('head', 'seq')
The draws below stay inside these ranges and needn't reach their ends.
All inputs are finite; a program needn't handle non-finite values.
Results may differ from the reference program's by a relative error of at most 0.015.
Values may be sent and summed in bfloat16 or wider, within the bound.
No kernel may reach another device: no remote copies, remote signals or barrier semaphores. Data moves between devices by JAX's collectives and lax.ppermute only.
A program may use at most 128 MiB of HBM per device.

```python
import jax
import jax.numpy as jnp
from jax import lax

D = 1024
HEADS = 8
DK = 128
FF = 2816
CONV = 4
GROUP = 64
SEQS = 1
TOK_DEV = 128
TOKENS = 1024
N_SEQ = 8


def level_of(key, extent, shards, low, top_value):
    factor_of = 1.0
    for axis_at, blocks in shards:
        steps = jax.random.uniform(jax.random.fold_in(jax.random.fold_in(key, 6), axis_at), (blocks,), jnp.float32, low / len(shards), top_value / len(shards))
        factor_of = factor_of * jnp.repeat(jnp.exp(steps), extent[axis_at] // blocks).reshape((-1,) + (1,) * (len(extent) - 1 - axis_at))
    return factor_of


def normal_values(stream_key, extent, scale, most, cuts=(), kind=jnp.bfloat16):
    result = jax.random.normal(stream_key, extent, jnp.float32) * scale
    if len(cuts) > 0:
        result = level_of(stream_key, extent, cuts, -0.22, 0.18) * result
    return jnp.clip(result, min=-most, max=most).astype(kind)


def setup_inputs(seed: int = 0) -> dict:
    streams_of = jax.random.split(jax.random.key(seed), 15)
    return {
        "block_input": normal_values(streams_of[0], (TOKENS, D), 1.0, 6.0, ((0, 8), (1, 4))),
        "mixer_gain": jnp.clip(1.0 + 0.1 * jax.random.normal(streams_of[1], (D,), jnp.float32), 0.5, 1.5).astype(jnp.bfloat16),
        "proj_weight": normal_values(streams_of[2], (D, HEADS, 4 * DK), D ** -0.5, 0.1875, ((1, 4),)),
        "rate_weight": normal_values(streams_of[3], (D, HEADS, 2), D ** -0.5, 0.1875, ((1, 4),)),
        "conv_weight": normal_values(streams_of[4], (CONV, HEADS, 3 * DK), 0.5, 3.0, ((1, 4),), jnp.float32),
        "decay_log": jnp.clip(-13.0 + 10.0 * jax.random.uniform(streams_of[5], (HEADS,), jnp.float32) ** level_of(streams_of[5], (HEADS,), ((0, 4),), -0.2, 0.2), -13.0, -3.0),
        "decay_bias": jnp.clip(-2.0 + 3.0 * jax.random.uniform(streams_of[6], (HEADS,), jnp.float32) ** level_of(streams_of[6], (HEADS,), ((0, 4),), -0.2, 0.2), -2.0, 1.0),
        "write_bias": jnp.clip(-6.0 + 4.0 * jax.random.uniform(streams_of[7], (HEADS,), jnp.float32) ** level_of(streams_of[7], (HEADS,), ((0, 4),), -0.2, 0.2), -6.0, -2.0),
        "output_gain": jnp.clip(1.0 + 0.1 * jax.random.normal(streams_of[8], (HEADS, DK), jnp.float32), 0.5, 1.5),
        "merge_weight": normal_values(streams_of[9], (HEADS * DK, D), (HEADS * DK // 4) ** -0.5, 0.375, ((0, 4),)),
        "feed_gain": jnp.clip(1.0 + 0.1 * jax.random.normal(streams_of[10], (D,), jnp.float32), 0.5, 1.5).astype(jnp.bfloat16),
        "gateup_weight": normal_values(streams_of[11], (D, 2, FF), D ** -0.5, 0.1875, ((2, 4),)),
        "down_weight": normal_values(streams_of[12], (FF, D), (FF // 4) ** -0.5, 0.21875, ((0, 4),)),
        "output_grad": normal_values(streams_of[13], (TOKENS, D), 1.0, 6.0, ((0, 8), (1, 4))),
    }


EPSILON = 1e-06
HIGH = lax.Precision.HIGHEST

def rms_scale(rows):
    return lax.rsqrt(lax.optimization_barrier(jnp.mean(rows * rows, axis=-1, keepdims=True)) + EPSILON)

def lower_solve(system, target):
    return jax.scipy.linalg.solve_triangular(system, target, lower=True, unit_diagonal=True)

def group_outputs(queries, key_rows, value_rows, write_rate, log_decay, memory):
    length = log_decay.shape[-1]
    position = jnp.arange(length)
    causal = position[None, :] <= position[:, None]
    strict = position[None, :] < position[:, None]
    cum_decay = jnp.cumsum(log_decay, axis=-1)
    decay_gap = cum_decay[:, :, None] - cum_decay[:, None, :]
    decays = jnp.where(causal, jnp.exp(jnp.where(causal, decay_gap, 0.0)), 0.0)
    key_inner = jnp.einsum('hcd,hsd->hcs', key_rows, key_rows, precision=HIGH)
    system = jnp.eye(length, dtype=jnp.float32) + jnp.where(strict, write_rate[:, :, None] * decays * key_inner, 0.0)
    growth = jnp.exp(cum_decay)
    weights = lower_solve(system, (write_rate * growth)[:, :, None] * key_rows)
    values = lower_solve(system, write_rate[:, :, None] * value_rows)
    remain = jnp.exp(cum_decay[:, -1:] - cum_decay)
    updates = values - jnp.einsum('hck,hvk->hcv', weights, memory, precision=HIGH)
    scores = decays * jnp.einsum('hcd,hsd->hcs', queries, key_rows, precision=HIGH)
    outputs = growth[:, :, None] * jnp.einsum('hck,hvk->hcv', queries, memory, precision=HIGH)
    outputs = outputs + jnp.einsum('hcs,hsv->hcv', scores, updates, precision=HIGH)
    memory_next = jnp.exp(cum_decay[:, -1])[:, None, None] * memory
    memory_next = memory_next + jnp.einsum('hcv,hc,hck->hvk', updates, remain, key_rows, precision=HIGH)
    return (outputs, memory_next)

def to_blocks(array):
    number = array.shape[0] // GROUP
    shaped = array.reshape((number, GROUP) + array.shape[1:])
    return jnp.moveaxis(shaped, 1, 2)

def run_memory(queries, key_rows, value_rows, write_rate, log_decay, memory):

    def advance(memory, pieces):
        outputs, memory_next = group_outputs(*pieces, memory)
        return (memory_next, outputs)
    blocks = tuple((to_blocks(element) for element in (queries, key_rows, value_rows, write_rate, log_decay)))
    memory_end, outputs = lax.scan(advance, memory, blocks)
    outputs = jnp.moveaxis(outputs, 2, 1).reshape(value_rows.shape)
    return (outputs, memory_end)

def front_part(extended, rates, conv_weight, decay_log, decay_bias, write_bias):
    length = rates.shape[0]
    kernel_taps = conv_weight.shape[0]
    mixed = extended[:length] * conv_weight[0]
    for offset in range(1, kernel_taps):
        mixed = mixed + extended[offset:offset + length] * conv_weight[offset]
    mixed = jax.nn.silu(mixed)
    head_dim = conv_weight.shape[-1] // 3
    queries = mixed[..., :head_dim]
    key_rows = mixed[..., head_dim:2 * head_dim]
    value_rows = mixed[..., 2 * head_dim:]
    queries = queries * lax.rsqrt(lax.optimization_barrier(jnp.sum(queries * queries, axis=-1, keepdims=True)) + EPSILON) * head_dim ** (-0.5)
    key_rows = key_rows * lax.rsqrt(lax.optimization_barrier(jnp.sum(key_rows * key_rows, axis=-1, keepdims=True)) + EPSILON)
    write_rate = jax.nn.sigmoid(rates[..., 0] + write_bias)
    log_decay = -jnp.exp(decay_log) * jax.nn.softplus(rates[..., 1] + decay_bias)
    return (queries, key_rows, value_rows, write_rate, log_decay)

def back_part(queries, key_rows, value_rows, write_rate, log_decay, gate_rows, output_gain, memory):
    outputs, memory_end = run_memory(queries, key_rows, value_rows, write_rate, log_decay, memory)
    normed = outputs * rms_scale(outputs) * output_gain * jax.nn.silu(gate_rows)
    return (normed, memory_end)

def reference(block_input, mixer_gain, proj_weight, rate_weight, conv_weight, decay_log, decay_bias, write_bias, output_gain, merge_weight, feed_gain, gateup_weight, down_weight, output_grad):
    inputs = block_input.astype(jnp.float32)
    scale_one = rms_scale(inputs)
    gain_one = mixer_gain.astype(jnp.float32)
    normed_in = (inputs * scale_one * gain_one).astype(jnp.bfloat16)
    normed_wide = normed_in.astype(jnp.float32)
    proj_wide = proj_weight.astype(jnp.float32)
    rate_wide = rate_weight.astype(jnp.float32)
    projected = jnp.einsum('td,dhe->the', normed_wide, proj_wide, precision=HIGH)
    conv_rows = projected[..., :3 * DK].astype(jnp.bfloat16)
    gate_rows = projected[..., 3 * DK:]
    rates = jnp.einsum('td,dhe->the', normed_wide, rate_wide, precision=HIGH)
    seq_length = TOKENS // SEQS
    padding = jnp.zeros((CONV - 1, HEADS, 3 * DK), jnp.float32)
    initial = jnp.zeros((HEADS, DK, DK), jnp.float32)

    def mixer(extended, rate_rows, gate_part, conv_taps, decay_scale, decay_shift, write_shift, norm_gain):
        features = front_part(extended, rate_rows, conv_taps, decay_scale, decay_shift, write_shift)
        normed, memory_end = back_part(*features, gate_part, norm_gain, initial)
        return normed
    normed_parts = []
    pullers = []
    for sequence in range(SEQS):
        first_row = sequence * seq_length
        extended = jnp.concatenate([padding, conv_rows[first_row:first_row + seq_length].astype(jnp.float32)], axis=0)
        normed, puller = jax.vjp(mixer, extended, rates[first_row:first_row + seq_length], gate_rows[first_row:first_row + seq_length], conv_weight, decay_log, decay_bias, write_bias, output_gain)
        normed_parts.append(normed)
        pullers.append(puller)
    mixed_rows = jnp.concatenate(normed_parts, axis=0).astype(jnp.bfloat16).reshape(TOKENS, HEADS * DK)
    mixer_out = jnp.dot(mixed_rows.astype(jnp.float32), merge_weight.astype(jnp.float32), preferred_element_type=jnp.float32)
    resid = inputs + mixer_out
    gain_two = feed_gain.astype(jnp.float32)
    gateup_wide = gateup_weight.astype(jnp.float32)

    def feed_block(carry, pieces):
        grad_gateup, grad_down, grad_gain = carry
        resid_rows, grad_rows = pieces
        scale_two = rms_scale(resid_rows)
        feed_in = (resid_rows * scale_two * gain_two).astype(jnp.bfloat16)
        feed_wide = feed_in.astype(jnp.float32)
        gateup = jnp.einsum('td,dcf->tcf', feed_wide, gateup_wide, precision=HIGH)
        gate_part = gateup[:, 0]
        up_part = gateup[:, 1]
        hidden = (jax.nn.silu(gate_part) * up_part).astype(jnp.bfloat16)
        block_rows = resid_rows + jnp.dot(hidden.astype(jnp.float32), down_weight.astype(jnp.float32), preferred_element_type=jnp.float32)
        grad_hidden = jnp.dot(grad_rows.astype(jnp.float32), down_weight.T.astype(jnp.float32), preferred_element_type=jnp.float32)
        grad_down = grad_down + jnp.dot(hidden.T.astype(jnp.float32), grad_rows.astype(jnp.float32), preferred_element_type=jnp.float32)
        sigma = jax.nn.sigmoid(gate_part)
        grad_gate = grad_hidden * up_part * sigma * (1.0 + gate_part * (1.0 - sigma))
        grad_up = grad_hidden * gate_part * sigma
        grad_gateup_rows = jnp.stack([grad_gate, grad_up], axis=1).astype(jnp.bfloat16).astype(jnp.float32)
        grad_gateup = grad_gateup + jnp.einsum('td,tcf->dcf', feed_wide, grad_gateup_rows, precision=HIGH)
        grad_feed_in = jnp.einsum('tcf,dcf->td', grad_gateup_rows, gateup_wide, precision=HIGH)
        grad_gain = grad_gain + lax.optimization_barrier(jnp.sum(grad_feed_in * resid_rows * scale_two, axis=0))
        weighted = grad_feed_in * gain_two
        grad_resid = grad_rows.astype(jnp.float32) + scale_two * weighted - resid_rows * scale_two ** 3 * lax.optimization_barrier(jnp.mean(weighted * resid_rows, axis=-1, keepdims=True))
        return ((grad_gateup, grad_down, grad_gain), (block_rows, grad_resid))
    starting = (jnp.zeros((D, 2, FF), jnp.float32), jnp.zeros((FF, D), jnp.float32), jnp.zeros((D,), jnp.float32))
    carried, produced = lax.scan(feed_block, starting, (resid.reshape(N_SEQ, TOK_DEV, D), output_grad.reshape(N_SEQ, TOK_DEV, D)))
    gateup_weight_grad, down_weight_grad, feed_gain_grad = carried
    block_output = produced[0].reshape(TOKENS, D)
    grad_resid = produced[1].reshape(TOKENS, D)
    grad_resid_half = grad_resid.astype(jnp.bfloat16)
    merge_weight_grad = jnp.dot(mixed_rows.T.astype(jnp.float32), grad_resid_half.astype(jnp.float32), preferred_element_type=jnp.float32)
    grad_mixed = jnp.dot(grad_resid_half.astype(jnp.float32), merge_weight.T.astype(jnp.float32), preferred_element_type=jnp.float32).reshape(TOKENS, HEADS, DK)
    conv_parts = []
    rate_parts = []
    gate_parts = []
    conv_weight_grad = jnp.zeros_like(conv_weight)
    decay_log_grad = jnp.zeros_like(decay_log)
    decay_bias_grad = jnp.zeros_like(decay_bias)
    write_bias_grad = jnp.zeros_like(write_bias)
    output_gain_grad = jnp.zeros_like(output_gain)
    for sequence in range(SEQS):
        first_row = sequence * seq_length
        grads = pullers[sequence](grad_mixed[first_row:first_row + seq_length])
        conv_parts.append(grads[0][CONV - 1:])
        rate_parts.append(grads[1])
        gate_parts.append(grads[2])
        conv_weight_grad = conv_weight_grad + grads[3]
        decay_log_grad = decay_log_grad + grads[4]
        decay_bias_grad = decay_bias_grad + grads[5]
        write_bias_grad = write_bias_grad + grads[6]
        output_gain_grad = output_gain_grad + grads[7]
    grad_conv_rows = jnp.concatenate(conv_parts, axis=0)
    grad_rates = jnp.concatenate(rate_parts, axis=0)
    grad_gate = jnp.concatenate(gate_parts, axis=0)
    grad_proj_rows = jnp.concatenate([grad_conv_rows, grad_gate], axis=-1).astype(jnp.bfloat16).astype(jnp.float32)
    grad_rates_half = grad_rates.astype(jnp.bfloat16).astype(jnp.float32)
    proj_weight_grad = jnp.einsum('td,the->dhe', normed_wide, grad_proj_rows, precision=HIGH)
    rate_weight_grad = jnp.einsum('td,the->dhe', normed_wide, grad_rates_half, precision=HIGH)
    grad_normed = jnp.einsum('the,dhe->td', grad_proj_rows, proj_wide, precision=HIGH)
    grad_normed = grad_normed + jnp.einsum('the,dhe->td', grad_rates_half, rate_wide, precision=HIGH)
    mixer_gain_grad = lax.optimization_barrier(jnp.sum(grad_normed * inputs * scale_one, axis=0))
    weighted = grad_normed * gain_one
    input_grad = grad_resid + scale_one * weighted - inputs * scale_one ** 3 * lax.optimization_barrier(jnp.mean(weighted * inputs, axis=-1, keepdims=True))
    return (block_output, input_grad, mixer_gain_grad, proj_weight_grad, rate_weight_grad, conv_weight_grad, decay_log_grad, decay_bias_grad, write_bias_grad, output_gain_grad, merge_weight_grad, feed_gain_grad, gateup_weight_grad, down_weight_grad)
```

```python
import functools

import jax
import jax.numpy as jnp
from jax import lax
from jax.experimental import pallas as pl
from jax.experimental.pallas import tpu as pltpu
from jax.sharding import PartitionSpec as P


EPSILON = 1e-06
EDGE = 8
BF = jnp.bfloat16
F32 = jnp.float32
NN = (((1,), (0,)), ((), ()))
NT = (((1,), (1,)), ((), ()))
TN = (((0,), (0,)), ((), ()))


def shifted(value, axis, steps):
    count = lax.axis_size(axis)
    pairs = [(i, i + steps) for i in range(count) if 0 <= i + steps < count]
    return lax.ppermute(value, axis, pairs)


def plane(ranks):
    inner = 1
    while inner * inner * 4 <= ranks:
        inner *= 2
    return ranks // inner, inner


def turned(value, axis, steps, group):
    count = lax.axis_size(axis)
    pairs = [(i, i // group * group + (i % group + steps) % group) for i in range(count)]
    return lax.ppermute(value, axis, pairs)


def in_group(value, ranks):
    _, inner = plane(ranks)
    return [value] + [turned(value, "seq", i, inner) for i in range(1, inner)]


def summed_over(value, axis):
    count = lax.axis_size(axis)
    step = 1
    while step < count:
        value = value + lax.ppermute(value, axis, [(i, i ^ step) for i in range(count)])
        step *= 2
    return value


def outer_sum(blocks, ranks):
    outer, inner = plane(ranks)
    total = blocks[0].astype(F32)
    for steps in range(1, outer):
        pairs = [(r, (r + steps * inner) % ranks) for r in range(ranks)]
        total = total + lax.ppermute(blocks[steps], "seq", pairs).astype(F32)
    return total


def rms_scale(rows):
    return lax.rsqrt(jnp.mean(rows * rows, axis=-1, keepdims=True) + EPSILON)


def halves(x):
    high = x.astype(BF)
    low = (x - high.astype(F32)).astype(BF)
    return high, low


def dot(a, b, dims=NN):
    ah, al = halves(a)
    bh, bl = halves(b)
    one = functools.partial(lax.dot_general, dimension_numbers=dims, preferred_element_type=F32)
    return one(ah, bh) + (one(ah, bl) + one(al, bh))


def grids(length):
    row = lax.broadcasted_iota(jnp.int32, (length, length), 0)
    col = lax.broadcasted_iota(jnp.int32, (length, length), 1)
    return row, col


def to_row(column, row, col):
    return jnp.sum(jnp.where(row == col, column, 0.0), axis=0, keepdims=True)


def to_column(line, row, col):
    return jnp.sum(jnp.where(row == col, line, 0.0), axis=1, keepdims=True)


def decay_matrix(cum, row, col):
    causal = col <= row
    gap = cum - to_row(cum, row, col)
    return jnp.where(causal, jnp.exp(jnp.where(causal, gap, 0.0)), 0.0)


def unit_lower_inverse(lower, row, col):
    length = lower.shape[0]
    identity = jnp.where(row == col, 1.0, 0.0)
    pair = (row // 2 == col // 2) & (col < row)
    inverse = identity - jnp.where(pair, lower, 0.0)
    size = 2
    while size < length:
        off = (row // (2 * size) == col // (2 * size)) & (row // size != col // size) & (col < row)
        inverse = inverse - dot(dot(inverse, jnp.where(off, lower, 0.0)), inverse)
        size *= 2
    return inverse


def setup_kernel(
    proj_ref, rates_ref, taps_ref, params_ref,
    pre_ref, q_ref, k_ref, inv_ref, w_ref, vals_ref, score_ref, inner_ref, cols_ref, map_ref,
    ext_ref,
):
    heads, rows, width = proj_ref.shape
    length = rows - EDGE
    dim = width // 4
    taps = taps_ref.shape[0]
    row, col = grids(length)
    for h in range(heads):
        ext_ref[...] = proj_ref[h, :, : 3 * dim].astype(BF).astype(F32)
        start = EDGE - taps + 1
        pre = ext_ref[start : start + length, :] * taps_ref[0, h : h + 1, :]
        for j in range(1, taps):
            pre = pre + ext_ref[start + j : start + j + length, :] * taps_ref[j, h : h + 1, :]
        pre_ref[h] = pre
        mixed = pre * jax.nn.sigmoid(pre)
        q = mixed[:, :dim]
        k = mixed[:, dim : 2 * dim]
        v = mixed[:, 2 * dim :]
        q = q * lax.rsqrt(jnp.sum(q * q, axis=1, keepdims=True) + EPSILON) * dim ** (-0.5)
        k = k * lax.rsqrt(jnp.sum(k * k, axis=1, keepdims=True) + EPSILON)
        beta = jax.nn.sigmoid(rates_ref[h, :, 0:1] + params_ref[2:3, h : h + 1])
        shift = rates_ref[h, :, 1:2] + params_ref[1:2, h : h + 1]
        soft = jnp.maximum(shift, 0.0) + jnp.log1p(jnp.exp(-jnp.abs(shift)))
        decay = -jnp.exp(params_ref[0:1, h : h + 1]) * soft
        cum = jnp.sum(jnp.where(col <= row, to_row(decay, row, col), 0.0), axis=1, keepdims=True)
        decays = decay_matrix(cum, row, col)
        growth = jnp.exp(cum)
        last = cum[length - 1 : length, :]
        remain = jnp.exp(last - cum)
        inner = jnp.where(col < row, decays * dot(k, k, NT), 0.0)
        inverse = unit_lower_inverse(beta * inner, row, col)
        weights = dot(inverse, (beta * growth) * k)
        values = dot(inverse, beta * v)
        kept = remain * k
        identity = jnp.where(row[:dim, :dim] == col[:dim, :dim], jnp.exp(last), 0.0)
        map_ref[0, h] = identity - dot(weights, kept, TN)
        map_ref[1, h] = dot(values, kept, TN)
        q_ref[h] = q
        k_ref[h] = k
        inv_ref[h] = inverse
        w_ref[h] = weights
        vals_ref[h] = values
        score_ref[h] = decays * dot(q, k, NT)
        inner_ref[h] = inner
        cols_ref[h] = jnp.concatenate(
            [cum, beta, decay, jax.nn.sigmoid(shift), jnp.zeros((length, 4), F32)], axis=1
        )


def outputs_kernel(
    q_ref, w_ref, vals_ref, score_ref, cols_ref, state_ref, gate_ref, gain_ref,
    mixed_ref, upd_ref, out_ref,
):
    heads, _, dim = q_ref.shape
    for h in range(heads):
        state = state_ref[h]
        upd = vals_ref[h] - dot(w_ref[h], state, NT)
        out = jnp.exp(cols_ref[h, :, 0:1]) * dot(q_ref[h], state, NT) + dot(score_ref[h], upd)
        gate = gate_ref[h, EDGE:, 3 * dim :]
        normed = out * lax.rsqrt(jnp.mean(out * out, axis=1, keepdims=True) + EPSILON)
        normed = normed * gain_ref[h : h + 1, :] * (gate * jax.nn.sigmoid(gate))
        mixed_ref[:, h * dim : (h + 1) * dim] = normed.astype(BF)
        upd_ref[h] = upd
        out_ref[h] = out


def local_back_kernel(
    grad_ref, out_ref, gate_ref, gain_ref, score_ref, q_ref, w_ref, cols_ref,
    dout_ref, dupd_ref, dstate_ref, dgate_ref, dgain_ref,
):
    heads, _, dim = q_ref.shape
    for h in range(heads):
        grad = grad_ref[:, h * dim : (h + 1) * dim]
        out = out_ref[h]
        scale = lax.rsqrt(jnp.mean(out * out, axis=1, keepdims=True) + EPSILON)
        normed = out * scale
        gate = gate_ref[h, EDGE:, 3 * dim :]
        sigma = jax.nn.sigmoid(gate)
        gain = gain_ref[h : h + 1, :]
        silu = gate * sigma
        dgain_ref[h : h + 1, :] = jnp.sum(grad * normed * silu, axis=0, keepdims=True)
        dgate_ref[h] = grad * normed * gain * (sigma * (1.0 + gate * (1.0 - sigma)))
        inside = grad * gain * silu
        dout = scale * (inside - normed * jnp.mean(inside * normed, axis=1, keepdims=True))
        dupd = dot(score_ref[h], dout, TN)
        grown = jnp.exp(cols_ref[h, :, 0:1]) * dout
        dstate_ref[h] = dot(grown, q_ref[h], TN) - dot(dupd, w_ref[h], TN)
        dout_ref[h] = dout
        dupd_ref[h] = dupd


def score_back_kernel(
    dout_ref, upd_ref, score_ref, q_ref, k_ref, cols_ref, state_ref,
    dq_ref, dk_ref, dcum_ref,
):
    heads, length, _ = q_ref.shape
    row, col = grids(length)
    for h in range(heads):
        dout = dout_ref[h]
        q = q_ref[h]
        cum = cols_ref[h, :, 0:1]
        dscore = jnp.where(col <= row, dot(dout, upd_ref[h], NT), 0.0)
        dinner = dscore * decay_matrix(cum, row, col)
        grown = dot(jnp.exp(cum) * dout, state_ref[h])
        dq_ref[h] = grown + dot(dinner, k_ref[h])
        dk_ref[h] = dot(dinner, q, TN)
        both = dscore * score_ref[h]
        dcum = jnp.sum(both, axis=1, keepdims=True) + jnp.sum(q * grown, axis=1, keepdims=True)
        dcum = dcum - to_column(jnp.sum(both, axis=0, keepdims=True), row, col)
        dcum_ref[h] = jnp.broadcast_to(dcum, (length, 8))


def final_back_kernel(
    dend_ref, dupd_ref, state_ref, upd_ref, inv_ref, inner_ref, k_ref, q_ref, cols_ref,
    dq_ref, dk_ref, dcum_ref, pre_ref, proj_ref, taps_ref, params_ref, dgate_ref,
    rows_ref, dtaps_ref, dparams_ref,
    ext_ref, pad_ref,
):
    heads, length, dim = q_ref.shape
    taps = taps_ref.shape[0]
    rows = length + EDGE
    row, col = grids(length)
    width = 4 * dim
    pad_ref[...] = jnp.zeros_like(pad_ref)
    rows_ref[:, heads * width :] = jnp.zeros((rows, rows_ref.shape[1] - heads * width), BF)
    lane = lax.broadcasted_iota(jnp.int32, (1, 128), 1)
    for h in range(heads):
        dend = dend_ref[h]
        state = state_ref[h]
        upd = upd_ref[h]
        k = k_ref[h]
        inner = inner_ref[h]
        cum = cols_ref[h, :, 0:1]
        beta = cols_ref[h, :, 1:2]
        decay = cols_ref[h, :, 2:3]
        soft_slope = cols_ref[h, :, 3:4]
        growth = jnp.exp(cum)
        last = cum[length - 1 : length, :]
        remain = jnp.exp(last - cum)
        kept = remain * k
        pre = pre_ref[h]
        sigma = jax.nn.sigmoid(pre)
        mixed = pre * sigma
        v = mixed[:, 2 * dim :]
        dupd = dupd_ref[h] + dot(kept, dend, NT)
        solved = dot(inv_ref[h], dupd, TN)
        dkept = dot(upd, dend)
        dright = -dot(solved, state)
        dlower = jnp.where(col < row, -dot(solved, upd, NT), 0.0)
        across = jnp.sum(dright * k, axis=1, keepdims=True)
        dlow_inner = dlower * inner
        dbeta_inner = jnp.sum(dlow_inner, axis=1, keepdims=True)
        dbeta = dbeta_inner + growth * across + jnp.sum(solved * v, axis=1, keepdims=True)
        both = beta * dlow_inner
        dinner = (dlower * beta) * decay_matrix(cum, row, col)
        dk = dk_ref[h] + dot(dinner, k) + dot(dinner, k, TN)
        dk = dk + (beta * growth) * dright + remain * dkept
        tail = jnp.sum(dkept * kept, axis=1, keepdims=True)
        dcum = dcum_ref[h, :, 0:1] + beta * dbeta_inner
        dcum = dcum - to_column(jnp.sum(both, axis=0, keepdims=True), row, col)
        dcum = dcum + (beta * growth) * across - tail
        dlast = jnp.sum(tail, axis=0, keepdims=True)
        held = jnp.sum(jnp.sum(state * dend, axis=1, keepdims=True), axis=0, keepdims=True)
        dlast = dlast + jnp.exp(last) * held
        ddecay = jnp.sum(jnp.where(col >= row, to_row(dcum, row, col), 0.0), axis=1, keepdims=True)
        ddecay = ddecay + dlast
        dv = beta * solved
        dshift = ddecay * (-jnp.exp(params_ref[0:1, h : h + 1])) * soft_slope
        dwrite = dbeta * beta * (1.0 - beta)
        total_log = jnp.sum(ddecay * decay, axis=0, keepdims=True)
        total_bias = jnp.sum(dshift, axis=0, keepdims=True)
        total_write = jnp.sum(dwrite, axis=0, keepdims=True)
        line = jnp.where(lane == 0, total_log, 0.0) + jnp.where(lane == 1, total_bias, 0.0)
        dparams_ref[h : h + 1, :] = line + jnp.where(lane == 2, total_write, 0.0)
        place = heads * width
        rate_lanes = jnp.where(lane == 2 * h, dwrite, 0.0) + jnp.where(lane == 2 * h + 1, dshift, 0.0)
        rows_ref[EDGE:, place : place + 128] += rate_lanes.astype(BF)
        q_raw = mixed[:, :dim]
        k_raw = mixed[:, dim : 2 * dim]
        q_scale = lax.rsqrt(jnp.sum(q_raw * q_raw, axis=1, keepdims=True) + EPSILON)
        k_scale = lax.rsqrt(jnp.sum(k_raw * k_raw, axis=1, keepdims=True) + EPSILON)
        q_unit = q_raw * q_scale
        dq = dq_ref[h] * dim ** (-0.5)
        dq = q_scale * (dq - q_unit * jnp.sum(dq * q_unit, axis=1, keepdims=True))
        dk = k_scale * (dk - k * jnp.sum(dk * k, axis=1, keepdims=True))
        slope = sigma * (1.0 + pre * (1.0 - sigma))
        dpre = jnp.concatenate([dq, dk, dv], axis=1) * slope
        pad_ref[EDGE : EDGE + length, :] = dpre
        ext_ref[...] = proj_ref[h, :, : 3 * dim].astype(BF).astype(F32)
        start = EDGE - taps + 1
        total = jnp.zeros((rows, 3 * dim), F32)
        for j in range(taps):
            dtaps_ref[j, h : h + 1, :] = jnp.sum(
                dpre * ext_ref[start + j : start + j + length, :], axis=0, keepdims=True
            )
            total = total + pad_ref[taps - 1 - j : taps - 1 - j + rows, :] * taps_ref[j, h : h + 1, :]
        rows_ref[:, h * width : h * width + 3 * dim] = total.astype(BF)
        rows_ref[:EDGE, h * width + 3 * dim : (h + 1) * width] = jnp.zeros((EDGE, dim), BF)
        rows_ref[EDGE:, h * width + 3 * dim : (h + 1) * width] = dgate_ref[h].astype(BF)


def picked(left, places, share):
    if share % 128 == 0:
        return left
    starts = [places[z] * share for z in range(places.shape[0])]
    return jnp.stack([lax.dynamic_slice_in_dim(left, start, share, 1) for start in starts])


def columns_of(left_ref, place_ref, z, share):
    if len(left_ref.shape) == 3:
        return left_ref[z]
    return left_ref[:, pl.ds(pl.multiple_of(place_ref[z] * share, share), share)]


def feature_minor_kernel(parts, lefts, which, place_ref, *refs):
    outer = place_ref.shape[0]
    rights = (len(refs) - outer) // parts - lefts
    for z in range(outer):
        out_ref = refs[len(refs) - outer + z]
        share = out_ref.shape[1]
        at = 0
        for a, b, i in which:
            total = None
            for p in range(parts):
                left = columns_of(refs[p * (lefts + rights) + a], place_ref, z, share)
                right = refs[p * (lefts + rights) + lefts + b][i]
                one = lax.dot_general(right, left, TN, preferred_element_type=F32)
                total = one if total is None else total + one
            out_ref[at : at + total.shape[0], :] = total.astype(BF)
            at += total.shape[0]


def feature_major_kernel(parts, place_ref, *refs):
    for z in range(place_ref.shape[0]):
        out_ref = refs[2 * parts + z]
        share = out_ref.shape[0]
        total = None
        for p in range(parts):
            left = columns_of(refs[2 * p], place_ref, z, share)
            one = lax.dot_general(left, refs[2 * p + 1][...], TN, preferred_element_type=F32)
            total = one if total is None else total + one
        out_ref[...] = total.astype(BF)


def input_back_kernel(rows_ref, weight_ref, inputs_ref, gain_ref, sent_ref):
    sides, rows, wide = sent_ref.shape
    local = wide - 128
    grad = lax.dot_general(rows_ref[...], weight_ref[...], NT, preferred_element_type=F32)
    stat = jnp.sum(grad * gain_ref[...] * inputs_ref[...], axis=1, keepdims=True)
    high, low = halves(stat)
    lane = lax.broadcasted_iota(jnp.int32, (rows, 128), 1)
    stats = jnp.where(lane == 0, high.astype(F32), 0.0) + jnp.where(lane == 1, low.astype(F32), 0.0)
    for side in range(sides):
        sent_ref[side, :, :local] = grad[:, side * local : (side + 1) * local].astype(BF)
        sent_ref[side, :, local:] = stats.astype(BF)


def compose_kernel(early_ref, late_ref, both_ref):
    for h in range(early_ref.shape[1]):
        later = late_ref[0, h]
        both_ref[0, h] = dot(early_ref[0, h], later)
        both_ref[1, h] = dot(early_ref[1, h], later) + late_ref[1, h]


def carry_kernel(first_ref, map_ref, second_ref, sum_ref):
    for h in range(first_ref.shape[0]):
        sum_ref[h] = dot(first_ref[h], map_ref[h]) + second_ref[h]


def carry_back_kernel(first_ref, map_ref, second_ref, sum_ref):
    for h in range(first_ref.shape[0]):
        sum_ref[h] = dot(first_ref[h], map_ref[h], NT) + second_ref[h]


def kernel_call(body, outs, args, dots, scratch=(), scalars=0):
    vmem = pl.BlockSpec(memory_space=pltpu.VMEM)
    smem = pl.BlockSpec(memory_space=pltpu.SMEM)
    shapes = [jax.ShapeDtypeStruct(shape, kind) for shape, kind in outs]
    total = sum(a.size * a.dtype.itemsize for a in args)
    return pl.pallas_call(
        body,
        out_shape=shapes,
        in_specs=[smem] * scalars + [vmem] * (len(args) - scalars),
        out_specs=[vmem] * len(outs),
        scratch_shapes=list(scratch),
        cost_estimate=pl.CostEstimate(
            flops=dots * 6 * 128**3, bytes_accessed=total, transcendentals=0
        ),
    )(*args)


def scan_states(pair, ranks, extras):
    heads = pair.shape[1]
    shape = pair.shape[1:]
    maps = []
    done = []
    span = 1
    while 2 * span < ranks:
        early = shifted(pair, "seq", span)
        joined = shifted(pair[0], "seq", 1 - span) if span > 1 else pair[0]
        if extras:
            early, joined, ready = lax.optimization_barrier((early, joined, extras[0]))
            extras = extras[1:]
            done.append(ready)
        else:
            early, joined = lax.optimization_barrier((early, joined))
        maps.append(joined)
        (pair,) = kernel_call(compose_kernel, [(pair.shape, F32)], (early, pair), 4 * heads)
        span *= 2
    near = shifted(pair, "seq", 1)
    if span + 1 >= ranks:
        return near[1], maps + [pair[0]], done + list(extras)
    far = shifted(pair[1], "seq", span + 1)
    joined = shifted(pair[0], "seq", -span)
    near, far, joined = lax.optimization_barrier((near, far, joined))
    (incoming,) = kernel_call(carry_kernel, [(shape, F32)], (far, near[0], near[1]), 2 * heads)
    return incoming, maps + [joined], done + list(extras)


def scan_back(local, maps, ranks, extra):
    heads = local.shape[0]
    total = local
    span = 1
    for level in range(len(maps) - 1):
        later = shifted(total, "seq", -span)
        if level == len(maps) - 2:
            later, extra = lax.optimization_barrier((later, extra))
        (total,) = kernel_call(
            carry_back_kernel, [(local.shape, F32)], (later, maps[level], total), 2 * heads
        )
        span *= 2
    near = shifted(total, "seq", -1)
    if span + 1 < ranks:
        far = shifted(total, "seq", -(span + 1))
        (near,) = kernel_call(
            carry_back_kernel, [(local.shape, F32)], (far, maps[-1], near), 2 * heads
        )
    return near, extra


def layer(
    block_input,
    mixer_gain,
    proj_weight,
    rate_weight,
    conv_weight,
    decay_log,
    decay_bias,
    write_bias,
    output_gain,
    merge_weight,
    feed_gain,
    gateup_weight,
    down_weight,
    output_grad,
):
    length, local_width = block_input.shape
    model_width, heads, width = proj_weight.shape
    dim = width // 4
    hidden_width = down_weight.shape[0]
    taps = conv_weight.shape[0]
    ranks = lax.axis_size("seq")
    sides = lax.axis_size("head")
    rank = lax.axis_index("seq")
    part = lax.axis_index("head")
    rows = length + EDGE

    edge = shifted(block_input[length - EDGE :], "seq", 1)
    gains = [jnp.broadcast_to(gain[None], (EDGE, local_width)) for gain in (mixer_gain, feed_gain)]
    packed = jnp.concatenate([edge, block_input, *gains, output_grad], axis=0)
    whole = lax.all_gather(packed, "head", axis=1, tiled=True)
    whole, merge_sent = lax.optimization_barrier((whole, merge_weight))
    inputs_ext = whole[:rows].astype(F32)
    inputs = inputs_ext[EDGE:]
    gain_one = whole[rows].astype(F32)
    gain_two = whole[rows + EDGE].astype(F32)
    grads_full = whole[rows + 2 * EDGE :]
    all_weight = jnp.concatenate(
        [merge_weight] + [turned(merge_sent, "head", i, sides) for i in range(1, sides)], axis=0
    )

    scale_ext = rms_scale(inputs_ext)
    normed_ext = (inputs_ext * scale_ext * gain_one).astype(BF)
    projected = jnp.einsum("td,dhe->hte", normed_ext, proj_weight, preferred_element_type=F32)
    rates = jnp.einsum(
        "td,dhe->hte", normed_ext[EDGE:], rate_weight, preferred_element_type=F32
    )
    params = jnp.stack([decay_log, decay_bias, write_bias])

    cube = (heads, length, dim)
    square = (heads, length, length)
    pre, q, k, inverse, weights, values, scores, inner, cols, pair = kernel_call(
        setup_kernel,
        [
            ((heads, length, 3 * dim), F32), (cube, F32), (cube, F32), (square, F32), (cube, F32),
            (cube, F32), (square, F32), (square, F32), ((heads, length, 8), F32),
            ((2, heads, dim, dim), F32),
        ],
        (projected, rates, conv_weight, params),
        18 * heads,
        [pltpu.VMEM((rows, 3 * dim), F32)],
    )
    rate_columns = jnp.moveaxis(rate_weight, 0, 2).reshape(2 * heads, model_width).T
    wide_weight = jnp.concatenate(
        [
            proj_weight.reshape(model_width, heads * width),
            jnp.pad(rate_columns, ((0, 0), (0, 128 - 2 * heads))),
        ],
        axis=1,
    )
    incoming, maps, (wide_weight, all_weight) = scan_states(pair, ranks, [wide_weight, all_weight])
    mixed_rows, updates, outs = kernel_call(
        outputs_kernel,
        [((length, heads * dim), BF), (cube, F32), (cube, F32)],
        (q, weights, values, scores, cols, incoming, projected, output_gain),
        3 * heads,
    )
    all_rows = jnp.concatenate(
        [mixed_rows] + [turned(mixed_rows, "head", i, sides) for i in range(1, sides)], axis=1
    )
    mixer_out = jnp.dot(all_rows, all_weight, preferred_element_type=F32)
    resid = inputs + mixer_out
    scale_two = rms_scale(resid)
    feed_in = (resid * scale_two * gain_two).astype(BF)
    gateup = jnp.einsum("td,dcf->tcf", feed_in, gateup_weight, preferred_element_type=F32)
    gate_part = gateup[:, 0]
    up_part = gateup[:, 1]
    sigma = jax.nn.sigmoid(gate_part)
    hidden = (gate_part * sigma * up_part).astype(BF)
    feed_part = jnp.dot(hidden, down_weight, preferred_element_type=F32)
    grad_hidden = jnp.einsum("td,fd->tf", grads_full, down_weight, preferred_element_type=F32)
    grad_gate = grad_hidden * up_part * sigma * (1.0 + gate_part * (1.0 - sigma))
    grad_up = grad_hidden * gate_part * sigma
    grad_gateup_rows = jnp.stack([grad_gate, grad_up], axis=0).astype(BF)
    grad_feed_part = jnp.einsum(
        "ctf,dcf->td", grad_gateup_rows, gateup_weight, preferred_element_type=F32
    )

    def by_side(value):
        return jnp.moveaxis(value.reshape(value.shape[0], sides, local_width), 1, 0)

    def by_part(values):
        return list(zip(*[in_group(value, ranks) for value in values]))

    feed_parts = by_part(
        [feed_in, grads_full, jnp.concatenate([grad_gateup_rows, hidden[None]], axis=0)]
    )
    got = lax.all_to_all(by_side(grad_feed_part.astype(BF)), "head", 0, 0, tiled=True)
    mine_feed_grad = jnp.sum(got.astype(F32), axis=0)
    got = lax.all_to_all(by_side(feed_part.astype(BF)), "head", 0, 0, tiled=True)
    feed_out = jnp.sum(got.astype(F32), axis=0)
    mine_resid = lax.dynamic_slice_in_dim(resid, part * local_width, local_width, 1)
    block_output = mine_resid + feed_out
    grad_feed_in = lax.all_gather(mine_feed_grad.astype(BF), "head", axis=1, tiled=True)
    grad_feed_in, feed_parts = lax.optimization_barrier((grad_feed_in, feed_parts))
    grad_feed_in = grad_feed_in.astype(F32)
    grad_gain_two = jnp.sum(mine_feed_grad * mine_resid * scale_two, axis=0)
    weighted = grad_feed_in * gain_two
    grad_resid = (
        grads_full.astype(F32)
        + scale_two * weighted
        - resid * scale_two**3 * jnp.mean(weighted * resid, axis=-1, keepdims=True)
    )
    grad_resid_half = grad_resid.astype(BF)
    grad_mixed = jnp.einsum("td,kd->tk", grad_resid_half, merge_weight, preferred_element_type=F32)

    douts, dupdates, dstate, dgate, grad_output_gain = kernel_call(
        local_back_kernel,
        [(cube, F32), (cube, F32), ((heads, dim, dim), F32), (cube, F32), ((heads, dim), F32)],
        (grad_mixed, outs, projected, output_gain, scores, q, weights, cols),
        3 * heads,
    )
    dq, dk, dcum = kernel_call(
        score_back_kernel,
        [(cube, F32), (cube, F32), ((heads, length, 8), F32)],
        (douts, updates, scores, q, k, cols, incoming),
        4 * heads,
    )

    share = model_width // ranks
    outer, group = plane(ranks)
    places = (rank // group + jnp.arange(outer)) % outer * group + rank % group

    merge_parts = by_part([grad_resid_half, mixed_rows[None]])
    parts = [
        [picked(left, places, share) for left in (feed[0], feed[1], merge[0])] + [feed[2], merge[1]]
        for feed, merge in zip(feed_parts, merge_parts)
    ]
    feed_rows = 3 * hidden_width
    late_blocks = kernel_call(
        functools.partial(
            feature_minor_kernel, len(parts), 3, ((0, 0, 0), (0, 0, 1), (1, 0, 2), (2, 1, 0))
        ),
        [((feed_rows + heads * dim, share), BF)] * outer,
        [places] + [ref for part_refs in parts for ref in part_refs],
        256,
        scalars=1,
    )
    grad_end, late_blocks = scan_back(dstate, maps, ranks, late_blocks)
    late_sum = outer_sum(late_blocks, ranks)
    feed_sum = late_sum[:feed_rows]
    grad_merge = late_sum[feed_rows:]
    grad_gateup = jnp.moveaxis(
        feed_sum[: 2 * hidden_width].reshape(2, hidden_width, share), 2, 0
    )
    grad_down = feed_sum[2 * hidden_width :]

    span_width = heads * width + 128
    grad_rows, grad_conv, grad_params = kernel_call(
        final_back_kernel,
        [((rows, span_width), BF), ((taps, heads, 3 * dim), F32), ((heads, 128), F32)],
        (
            grad_end, dupdates, incoming, updates, inverse, inner, k, q, cols, dq, dk, dcum,
            pre, projected, conv_weight, params, dgate,
        ),
        7 * heads,
        [pltpu.VMEM((rows, 3 * dim), F32), pltpu.VMEM((rows + EDGE, 3 * dim), F32)],
    )
    right_parts = in_group(grad_rows, ranks)
    left_parts = [picked(left, places, share) for left in in_group(normed_ext, ranks)]
    parts = list(zip(left_parts, right_parts))
    blocks = kernel_call(
        functools.partial(feature_major_kernel, len(parts)),
        [((share, span_width), BF)] * outer,
        [places] + [ref for part_refs in parts for ref in part_refs],
        100,
        scalars=1,
    )
    summed_rows = outer_sum(blocks, ranks)
    (sent,) = kernel_call(
        input_back_kernel,
        [((sides, rows, local_width + 128), BF)],
        (grad_rows, wide_weight, inputs_ext, gain_one[None]),
        64,
    )
    got = lax.all_to_all(sent, "head", 0, 0, tiled=True)
    got = jnp.sum(got.astype(F32), axis=0)
    mine_normed = got[:, :local_width]
    stat_total = got[:, local_width : local_width + 1] + got[:, local_width + 1 : local_width + 2]
    mine_ext = lax.dynamic_slice_in_dim(inputs_ext, part * local_width, local_width, 1)
    mine_gain = lax.dynamic_slice_in_dim(gain_one, part * local_width, local_width, 0)
    grad_gain_one = jnp.sum(mine_normed * mine_ext * scale_ext, axis=0)
    input_part = (
        scale_ext * mine_normed * mine_gain
        - mine_ext * scale_ext**3 * (stat_total / model_width)
    )
    from_next = shifted(input_part[:EDGE], "seq", -1)
    mine_resid_grad = lax.dynamic_slice_in_dim(grad_resid, part * local_width, local_width, 1)
    input_grad = mine_resid_grad + input_part[EDGE:]
    input_grad = jnp.concatenate(
        [input_grad[: length - EDGE], input_grad[length - EDGE :] + from_next], axis=0
    )

    small = [
        grad_conv.reshape(-1, 128),
        grad_output_gain.reshape(-1, 128),
        grad_params,
        grad_gain_two.reshape(-1, 128),
        grad_gain_one.reshape(-1, 128),
    ]
    ends = [0]
    for piece in small:
        ends.append(ends[-1] + piece.shape[0])
    total = summed_over(jnp.concatenate(small, axis=0), "seq")
    small = [total[start:end] for start, end in zip(ends, ends[1:])]
    conv_split = 3 * dim // ranks
    gain_split = dim // ranks
    grad_conv_mine = lax.dynamic_slice_in_dim(
        small[0].reshape(taps, heads, 3 * dim), rank * conv_split, conv_split, 2
    )
    grad_output_gain_mine = lax.dynamic_slice_in_dim(
        small[1].reshape(heads, dim), rank * gain_split, gain_split, 1
    )
    grad_params = small[2]
    grad_gain_two = small[3].reshape(-1)
    grad_gain_one = small[4].reshape(-1)
    grad_proj_mine = summed_rows[:, : heads * width].reshape(share, heads, width)
    grad_rate_mine = summed_rows[:, heads * width : heads * (width + 2)].reshape(share, heads, 2)
    return (
        block_output,
        input_grad,
        grad_gain_one,
        grad_proj_mine,
        grad_rate_mine,
        grad_conv_mine,
        grad_params[:, 0],
        grad_params[:, 1],
        grad_params[:, 2],
        grad_output_gain_mine,
        grad_merge,
        grad_gain_two,
        grad_gateup,
        grad_down,
    )


def solution(mesh):
    return jax.shard_map(
        layer,
        mesh=mesh,
        in_specs=(
            P("seq", "head"),
            P("head"),
            P(None, "head", None),
            P(None, "head", None),
            P(None, "head", None),
            P("head"),
            P("head"),
            P("head"),
            P("head", None),
            P("head", None),
            P("head"),
            P(None, None, "head"),
            P("head", None),
            P("seq", "head"),
        ),
        out_specs=(
            P("seq", "head"),
            P("seq", "head"),
            P("head"),
            P("seq", "head", None),
            P("seq", "head", None),
            P(None, "head", "seq"),
            P("head"),
            P("head"),
            P("head"),
            P("head", "seq"),
            P("head", "seq"),
            P("head"),
            P("seq", None, "head"),
            P("head", "seq"),
        ),
        check_vma=False,
    )
```

```python
import functools

import jax
import jax.numpy as jnp
from jax import lax
from jax.experimental import pallas as pl
from jax.experimental.pallas import tpu as pltpu
from jax.sharding import PartitionSpec as P


EPSILON = 1e-06
EDGE = 8
BF = jnp.bfloat16
F32 = jnp.float32
NN = (((1,), (0,)), ((), ()))
NT = (((1,), (1,)), ((), ()))
TN = (((0,), (0,)), ((), ()))


def shifted(value, axis, steps):
    count = lax.axis_size(axis)
    pairs = [(i, i + steps) for i in range(count) if 0 <= i + steps < count]
    return lax.ppermute(value, axis, pairs)


def plane(ranks):
    inner = 1
    while inner * inner * 4 <= ranks:
        inner *= 2
    return ranks // inner, inner


def turned(value, axis, steps, group):
    count = lax.axis_size(axis)
    pairs = [(i, i // group * group + (i % group + steps) % group) for i in range(count)]
    return lax.ppermute(value, axis, pairs)


def in_group(value, ranks):
    _, inner = plane(ranks)
    return [value] + [turned(value, "seq", i, inner) for i in range(1, inner)]


def shared_sum(value, ranks):
    outer, inner = plane(ranks)
    step = 1
    while step < inner:
        other = lax.ppermute(value, "seq", [(i, i ^ step) for i in range(ranks)])
        value = value + other
        step *= 2
    return [value] + [outward(value, ranks, steps) for steps in range(1, outer)]


def ordered_sum(parts, place):
    stacked = jnp.stack(parts)
    count = len(parts)
    return sum(
        lax.dynamic_index_in_dim(stacked, (place - i) % count, 0, keepdims=False)
        for i in range(count)
    )


def outward(value, ranks, steps):
    _, inner = plane(ranks)
    pairs = [(r, (r + steps * inner) % ranks) for r in range(ranks)]
    return lax.ppermute(value, "seq", pairs)


def inner_sum(blocks, ranks):
    _, inner = plane(ranks)
    total = blocks[0].astype(F32)
    for steps in range(1, inner):
        total = total + turned(blocks[steps], "seq", steps, inner).astype(F32)
    return total


def rms_scale(rows):
    return lax.rsqrt(jnp.mean(rows * rows, axis=-1, keepdims=True) + EPSILON)


def halves(x):
    high = x.astype(BF)
    low = (x - high.astype(F32)).astype(BF)
    return high, low


def dot(a, b, dims=NN):
    ah, al = halves(a)
    bh, bl = halves(b)
    one = functools.partial(lax.dot_general, dimension_numbers=dims, preferred_element_type=F32)
    return one(ah, bh) + (one(ah, bl) + one(al, bh))


def grids(length):
    row = lax.broadcasted_iota(jnp.int32, (length, length), 0)
    col = lax.broadcasted_iota(jnp.int32, (length, length), 1)
    return row, col


def to_row(column, row, col):
    return jnp.sum(jnp.where(row == col, column, 0.0), axis=0, keepdims=True)


def to_column(line, row, col):
    return jnp.sum(jnp.where(row == col, line, 0.0), axis=1, keepdims=True)


def decay_matrix(cum, row, col):
    causal = col <= row
    gap = cum - to_row(cum, row, col)
    return jnp.where(causal, jnp.exp(jnp.where(causal, gap, 0.0)), 0.0)


def unit_lower_inverse(lower, row, col):
    length = lower.shape[0]
    identity = jnp.where(row == col, 1.0, 0.0)
    pair = (row // 2 == col // 2) & (col < row)
    inverse = identity - jnp.where(pair, lower, 0.0)
    size = 2
    while size < length:
        off = (row // (2 * size) == col // (2 * size)) & (row // size != col // size) & (col < row)
        inverse = inverse - dot(dot(inverse, jnp.where(off, lower, 0.0)), inverse)
        size *= 2
    return inverse


def pack_kernel(edge_ref, input_ref, gains_ref, grad_ref, packed_ref):
    length, _ = input_ref.shape
    rows = length + EDGE
    packed_ref[:EDGE, :] = edge_ref[...]
    packed_ref[EDGE:rows, :] = input_ref[...]
    packed_ref[rows : rows + 2 * EDGE, :] = gains_ref[...]
    packed_ref[rows + 2 * EDGE :, :] = grad_ref[...]


def setup_kernel(
    proj_ref, rates_ref, taps_ref, params_ref,
    pre_ref, q_ref, k_ref, inv_ref, w_ref, vals_ref, score_ref, inner_ref, cols_ref, map_ref, alone_ref, offset_ref,
    ext_ref,
):
    heads, rows, width = proj_ref.shape
    length = rows - EDGE
    dim = width // 4
    taps = taps_ref.shape[0]
    row, col = grids(length)
    for h in range(heads):
        ext_ref[...] = proj_ref[h, :, : 3 * dim].astype(BF).astype(F32)
        start = EDGE - taps + 1
        pre = ext_ref[start : start + length, :] * taps_ref[0, h : h + 1, :]
        for j in range(1, taps):
            pre = pre + ext_ref[start + j : start + j + length, :] * taps_ref[j, h : h + 1, :]
        pre_ref[h] = pre
        mixed = pre * jax.nn.sigmoid(pre)
        q = mixed[:, :dim]
        k = mixed[:, dim : 2 * dim]
        v = mixed[:, 2 * dim :]
        q = q * lax.rsqrt(jnp.sum(q * q, axis=1, keepdims=True) + EPSILON) * dim ** (-0.5)
        k = k * lax.rsqrt(jnp.sum(k * k, axis=1, keepdims=True) + EPSILON)
        beta = jax.nn.sigmoid(rates_ref[h, :, 0:1] + params_ref[2:3, h : h + 1])
        shift = rates_ref[h, :, 1:2] + params_ref[1:2, h : h + 1]
        soft = jnp.maximum(shift, 0.0) + jnp.log1p(jnp.exp(-jnp.abs(shift)))
        decay = -jnp.exp(params_ref[0:1, h : h + 1]) * soft
        cum = jnp.sum(jnp.where(col <= row, to_row(decay, row, col), 0.0), axis=1, keepdims=True)
        decays = decay_matrix(cum, row, col)
        growth = jnp.exp(cum)
        last = cum[length - 1 : length, :]
        remain = jnp.exp(last - cum)
        inner = jnp.where(col < row, decays * dot(k, k, NT), 0.0)
        inverse = unit_lower_inverse(beta * inner, row, col)
        weights = dot(inverse, (beta * growth) * k)
        values = dot(inverse, beta * v)
        kept = remain * k
        identity = jnp.where(row[:dim, :dim] == col[:dim, :dim], jnp.exp(last), 0.0)
        alone = identity - dot(weights, kept, TN)
        offset = dot(values, kept, TN)
        map_ref[0, h] = alone
        map_ref[1, h] = offset
        alone_ref[h] = alone
        offset_ref[h] = offset
        q_ref[h] = q
        k_ref[h] = k
        inv_ref[h] = inverse
        w_ref[h] = weights
        vals_ref[h] = values
        score_ref[h] = decays * dot(q, k, NT)
        inner_ref[h] = inner
        cols_ref[h] = jnp.concatenate(
            [cum, beta, decay, jax.nn.sigmoid(shift), jnp.zeros((length, 4), F32)], axis=1
        )


def outputs_kernel(
    q_ref, w_ref, vals_ref, score_ref, cols_ref, state_ref, gate_ref, gain_ref,
    mixed_ref, upd_ref, out_ref,
):
    heads, _, dim = q_ref.shape
    for h in range(heads):
        state = state_ref[h]
        upd = vals_ref[h] - dot(w_ref[h], state, NT)
        out = jnp.exp(cols_ref[h, :, 0:1]) * dot(q_ref[h], state, NT) + dot(score_ref[h], upd)
        gate = gate_ref[h, EDGE:, 3 * dim :]
        normed = out * lax.rsqrt(jnp.mean(out * out, axis=1, keepdims=True) + EPSILON)
        normed = normed * gain_ref[h : h + 1, :] * (gate * jax.nn.sigmoid(gate))
        mixed_ref[:, h * dim : (h + 1) * dim] = normed.astype(BF)
        upd_ref[h] = upd
        out_ref[h] = out


def feed_kernel(sides, place_ref, whole_ref, gateup_ref, down_ref, *refs):
    rows_refs, merge_refs = refs[:sides], refs[sides : 2 * sides]
    resid_ref, right_ref, sent_ref, back_ref, back_half_ref, *feed_refs = refs[2 * sides :]
    feed_ref = feed_refs.pop()
    length = resid_ref.shape[0]
    rows = length + EDGE
    hidden = down_ref.shape[0]
    resid = whole_ref[EDGE:rows, :].astype(F32)
    for row_ref, merge_ref in zip(rows_refs, merge_refs):
        resid = resid + jnp.dot(row_ref[...], merge_ref[...], preferred_element_type=F32)
    resid_ref[...] = resid
    gain = whole_ref[rows + EDGE : rows + EDGE + 1, :].astype(F32)
    feed_in = (resid * rms_scale(resid) * gain).astype(BF)
    feed_ref[...] = feed_in
    for i, pick_ref in enumerate(feed_refs):
        pick_ref[...] = columns_of(feed_ref, place_ref, i, pick_ref.shape[1])
    one = functools.partial(lax.dot_general, preferred_element_type=F32)
    gate = one(gateup_ref[0], feed_in, NT)
    up = one(gateup_ref[1], feed_in, NT)
    grad_hidden = one(down_ref[...], whole_ref[rows + 2 * EDGE :, :], NT)
    sigma = jax.nn.sigmoid(gate)
    active = (gate * sigma * up).astype(BF)
    grad_gate = (grad_hidden * up * sigma * (1.0 + gate * (1.0 - sigma))).astype(BF)
    grad_up = (grad_hidden * gate * sigma).astype(BF)
    right_ref[:hidden, :] = grad_gate
    right_ref[hidden : 2 * hidden, :] = grad_up
    right_ref[2 * hidden :, :] = active
    back = one(grad_gate, gateup_ref[0], TN) + one(grad_up, gateup_ref[1], TN)
    back_ref[...] = back
    back_half_ref[...] = back.astype(BF)
    out = one(active, down_ref[...], TN).astype(BF)
    local = out.shape[1] // sides
    for side in range(sides):
        sent_ref[side] = out[:, side * local : (side + 1) * local]


def resid_back_kernel(
    others, whole_ref, resid_ref, merge_ref, out_ref, gate_ref, gain_ref, score_ref, q_ref, w_ref,
    cols_ref, back_ref, *refs,
):
    (
        grad_ref, half_ref, dfeed_ref, dout_ref, dupd_ref, dstate_ref, dgate_ref, dgain_ref,
    ) = refs[others:]
    heads, length, dim = q_ref.shape
    rows = length + EDGE
    back = back_ref[...]
    for other_ref in refs[:others]:
        back = back + other_ref[...].astype(F32)
    resid = resid_ref[...]
    scale = rms_scale(resid)
    dfeed_ref[...] = jnp.sum(back * resid * scale, axis=0, keepdims=True)
    weighted = back * whole_ref[rows + EDGE : rows + EDGE + 1, :].astype(F32)
    grad = whole_ref[rows + 2 * EDGE :, :].astype(F32) + scale * weighted
    grad = grad - resid * (scale * scale * scale) * jnp.mean(
        weighted * resid, axis=1, keepdims=True
    )
    grad_ref[...] = grad
    half = grad.astype(BF)
    half_ref[...] = half
    grad_mixed = lax.dot_general(half, merge_ref[...], NT, preferred_element_type=F32)
    for h in range(heads):
        grad = grad_mixed[:, h * dim : (h + 1) * dim]
        out = out_ref[h]
        scale = lax.rsqrt(jnp.mean(out * out, axis=1, keepdims=True) + EPSILON)
        normed = out * scale
        gate = gate_ref[h, EDGE:, 3 * dim :]
        sigma = jax.nn.sigmoid(gate)
        gain = gain_ref[h : h + 1, :]
        silu = gate * sigma
        dgain_ref[h : h + 1, :] = jnp.sum(grad * normed * silu, axis=0, keepdims=True)
        dgate_ref[h] = grad * normed * gain * (sigma * (1.0 + gate * (1.0 - sigma)))
        inside = grad * gain * silu
        dout = scale * (inside - normed * jnp.mean(inside * normed, axis=1, keepdims=True))
        dupd = dot(score_ref[h], dout, TN)
        grown = jnp.exp(cols_ref[h, :, 0:1]) * dout
        dstate_ref[h] = dot(grown, q_ref[h], TN) - dot(dupd, w_ref[h], TN)
        dout_ref[h] = dout
        dupd_ref[h] = dupd


def score_back_kernel(
    dout_ref, upd_ref, score_ref, q_ref, k_ref, cols_ref, state_ref,
    dq_ref, dk_ref, dcum_ref,
):
    heads, length, _ = q_ref.shape
    row, col = grids(length)
    for h in range(heads):
        dout = dout_ref[h]
        q = q_ref[h]
        cum = cols_ref[h, :, 0:1]
        dscore = jnp.where(col <= row, dot(dout, upd_ref[h], NT), 0.0)
        dinner = dscore * decay_matrix(cum, row, col)
        grown = dot(jnp.exp(cum) * dout, state_ref[h])
        dq_ref[h] = grown + dot(dinner, k_ref[h])
        dk_ref[h] = dot(dinner, q, TN)
        both = dscore * score_ref[h]
        dcum = jnp.sum(both, axis=1, keepdims=True) + jnp.sum(q * grown, axis=1, keepdims=True)
        dcum = dcum - to_column(jnp.sum(both, axis=0, keepdims=True), row, col)
        dcum_ref[h] = jnp.broadcast_to(dcum, (length, 8))


def final_back_kernel(
    dend_ref, dupd_ref, state_ref, upd_ref, inv_ref, inner_ref, k_ref, q_ref, cols_ref,
    dq_ref, dk_ref, dcum_ref, pre_ref, proj_ref, taps_ref, params_ref, dgate_ref,
    rows_ref, dtaps_ref, dparams_ref,
    ext_ref, pad_ref,
):
    heads, length, dim = q_ref.shape
    taps = taps_ref.shape[0]
    rows = length + EDGE
    row, col = grids(length)
    width = 4 * dim
    pad_ref[...] = jnp.zeros_like(pad_ref)
    rows_ref[:, heads * width :] = jnp.zeros((rows, rows_ref.shape[1] - heads * width), BF)
    lane = lax.broadcasted_iota(jnp.int32, (1, 128), 1)
    for h in range(heads):
        dend = dend_ref[h]
        state = state_ref[h]
        upd = upd_ref[h]
        k = k_ref[h]
        inner = inner_ref[h]
        cum = cols_ref[h, :, 0:1]
        beta = cols_ref[h, :, 1:2]
        decay = cols_ref[h, :, 2:3]
        soft_slope = cols_ref[h, :, 3:4]
        growth = jnp.exp(cum)
        last = cum[length - 1 : length, :]
        remain = jnp.exp(last - cum)
        kept = remain * k
        pre = pre_ref[h]
        sigma = jax.nn.sigmoid(pre)
        mixed = pre * sigma
        v = mixed[:, 2 * dim :]
        dupd = dupd_ref[h] + dot(kept, dend, NT)
        solved = dot(inv_ref[h], dupd, TN)
        dkept = dot(upd, dend)
        dright = -dot(solved, state)
        dlower = jnp.where(col < row, -dot(solved, upd, NT), 0.0)
        across = jnp.sum(dright * k, axis=1, keepdims=True)
        dlow_inner = dlower * inner
        dbeta_inner = jnp.sum(dlow_inner, axis=1, keepdims=True)
        dbeta = dbeta_inner + growth * across + jnp.sum(solved * v, axis=1, keepdims=True)
        both = beta * dlow_inner
        dinner = (dlower * beta) * decay_matrix(cum, row, col)
        dk = dk_ref[h] + dot(dinner, k) + dot(dinner, k, TN)
        dk = dk + (beta * growth) * dright + remain * dkept
        tail = jnp.sum(dkept * kept, axis=1, keepdims=True)
        dcum = dcum_ref[h, :, 0:1] + beta * dbeta_inner
        dcum = dcum - to_column(jnp.sum(both, axis=0, keepdims=True), row, col)
        dcum = dcum + (beta * growth) * across - tail
        dlast = jnp.sum(tail, axis=0, keepdims=True)
        held = jnp.sum(jnp.sum(state * dend, axis=1, keepdims=True), axis=0, keepdims=True)
        dlast = dlast + jnp.exp(last) * held
        ddecay = jnp.sum(jnp.where(col >= row, to_row(dcum, row, col), 0.0), axis=1, keepdims=True)
        ddecay = ddecay + dlast
        dv = beta * solved
        dshift = ddecay * (-jnp.exp(params_ref[0:1, h : h + 1])) * soft_slope
        dwrite = dbeta * beta * (1.0 - beta)
        total_log = jnp.sum(ddecay * decay, axis=0, keepdims=True)
        total_bias = jnp.sum(dshift, axis=0, keepdims=True)
        total_write = jnp.sum(dwrite, axis=0, keepdims=True)
        line = jnp.where(lane == 0, total_log, 0.0) + jnp.where(lane == 1, total_bias, 0.0)
        dparams_ref[h : h + 1, :] = line + jnp.where(lane == 2, total_write, 0.0)
        place = heads * width
        rate_lanes = jnp.where(lane == 2 * h, dwrite, 0.0) + jnp.where(lane == 2 * h + 1, dshift, 0.0)
        rows_ref[EDGE:, place : place + 128] += rate_lanes.astype(BF)
        q_raw = mixed[:, :dim]
        k_raw = mixed[:, dim : 2 * dim]
        q_scale = lax.rsqrt(jnp.sum(q_raw * q_raw, axis=1, keepdims=True) + EPSILON)
        k_scale = lax.rsqrt(jnp.sum(k_raw * k_raw, axis=1, keepdims=True) + EPSILON)
        q_unit = q_raw * q_scale
        dq = dq_ref[h] * dim ** (-0.5)
        dq = q_scale * (dq - q_unit * jnp.sum(dq * q_unit, axis=1, keepdims=True))
        dk = k_scale * (dk - k * jnp.sum(dk * k, axis=1, keepdims=True))
        slope = sigma * (1.0 + pre * (1.0 - sigma))
        dpre = jnp.concatenate([dq, dk, dv], axis=1) * slope
        pad_ref[EDGE : EDGE + length, :] = dpre
        ext_ref[...] = proj_ref[h, :, : 3 * dim].astype(BF).astype(F32)
        start = EDGE - taps + 1
        total = jnp.zeros((rows, 3 * dim), F32)
        for j in range(taps):
            dtaps_ref[j, h : h + 1, :] = jnp.sum(
                dpre * ext_ref[start + j : start + j + length, :], axis=0, keepdims=True
            )
            total = total + pad_ref[taps - 1 - j : taps - 1 - j + rows, :] * taps_ref[j, h : h + 1, :]
        rows_ref[:, h * width : h * width + 3 * dim] = total.astype(BF)
        rows_ref[:EDGE, h * width + 3 * dim : (h + 1) * width] = jnp.zeros((EDGE, dim), BF)
        rows_ref[EDGE:, h * width + 3 * dim : (h + 1) * width] = dgate_ref[h].astype(BF)


def picked(left, places, share):
    if share % 128 == 0:
        return left
    starts = [places[z] * share for z in range(places.shape[0])]
    return jnp.stack([lax.dynamic_slice_in_dim(left, start, share, 1) for start in starts])


def columns_of(left_ref, place_ref, z, share):
    if len(left_ref.shape) == 3:
        return left_ref[z]
    return left_ref[:, pl.ds(pl.multiple_of(place_ref[z] * share, share), share)]


def blocks_kernel(parts, lefts, which, dims, place_ref, *refs):
    outer = place_ref.shape[0]
    rights = (len(refs) - outer) // parts - lefts
    for z in range(outer):
        out_ref = refs[len(refs) - outer + z]
        share = out_ref.shape[1]
        at = 0
        for a, b in which:
            total = None
            for p in range(parts):
                left = columns_of(refs[p * (lefts + rights) + a], place_ref, z, share)
                right_ref = refs[p * (lefts + rights) + lefts + b[0]]
                right = right_ref[b[1] : b[2], :] if len(b) > 1 else right_ref[...]
                one = lax.dot_general(right, left, dims, preferred_element_type=F32)
                total = one if total is None else total + one
            out_ref[at : at + total.shape[0], :] = total.astype(BF)
            at += total.shape[0]


def feature_major_kernel(parts, place_ref, *refs):
    for z in range(place_ref.shape[0]):
        out_ref = refs[2 * parts + z]
        share = out_ref.shape[0]
        total = None
        for p in range(parts):
            left = columns_of(refs[2 * p], place_ref, z, share)
            one = lax.dot_general(left, refs[2 * p + 1][...], TN, preferred_element_type=F32)
            total = one if total is None else total + one
        out_ref[...] = total.astype(BF)


def input_back_kernel(rows_ref, weight_ref, inputs_ref, gain_ref, sent_ref):
    sides, rows, wide = sent_ref.shape
    local = wide - 128
    grad = lax.dot_general(rows_ref[...], weight_ref[...], NT, preferred_element_type=F32)
    stat = jnp.sum(grad * gain_ref[...] * inputs_ref[...], axis=1, keepdims=True)
    high, low = halves(stat)
    lane = lax.broadcasted_iota(jnp.int32, (rows, 128), 1)
    stats = jnp.where(lane == 0, high.astype(F32), 0.0) + jnp.where(lane == 1, low.astype(F32), 0.0)
    for side in range(sides):
        sent_ref[side, :, :local] = grad[:, side * local : (side + 1) * local].astype(BF)
        sent_ref[side, :, local:] = stats.astype(BF)


def compose_kernel(early_ref, late_ref, both_ref, alone_ref, offset_ref):
    for h in range(early_ref.shape[1]):
        later = late_ref[0, h]
        alone = dot(early_ref[0, h], later)
        offset = dot(early_ref[1, h], later) + late_ref[1, h]
        both_ref[0, h] = alone
        both_ref[1, h] = offset
        alone_ref[h] = alone
        offset_ref[h] = offset


def carry_kernel(first_ref, pair_ref, sum_ref):
    for h in range(first_ref.shape[0]):
        sum_ref[h] = dot(first_ref[h], pair_ref[0, h]) + pair_ref[1, h]


def carry_back_kernel(first_ref, map_ref, second_ref, sum_ref):
    for h in range(first_ref.shape[0]):
        sum_ref[h] = dot(first_ref[h], map_ref[h], NT) + second_ref[h]


def kernel_call(body, outs, args, dots, scratch=(), scalars=0):
    vmem = pl.BlockSpec(memory_space=pltpu.VMEM)
    smem = pl.BlockSpec(memory_space=pltpu.SMEM)
    shapes = [jax.ShapeDtypeStruct(shape, kind) for shape, kind in outs]
    total = sum(a.size * a.dtype.itemsize for a in args)
    return pl.pallas_call(
        body,
        out_shape=shapes,
        in_specs=[smem] * scalars + [vmem] * (len(args) - scalars),
        out_specs=[vmem] * len(outs),
        scratch_shapes=list(scratch),
        cost_estimate=pl.CostEstimate(
            flops=dots * 6 * 128**3, bytes_accessed=total, transcendentals=0
        ),
    )(*args)


def scan_states(pair, alone, offset, ranks, extras):
    heads = pair.shape[1]
    shape = (pair.shape[1:], F32)
    maps = []
    done = []
    span = 1
    while 2 * span < ranks:
        early = shifted(pair, "seq", span)
        joined = shifted(alone, "seq", 1 - span) if span > 1 else alone
        if extras:
            early, joined, ready = lax.optimization_barrier((early, joined, extras[0]))
            extras = extras[1:]
            done.append(ready)
        else:
            early, joined = lax.optimization_barrier((early, joined))
        maps.append(joined)
        pair, alone, offset = kernel_call(
            compose_kernel, [(pair.shape, F32), shape, shape], (early, pair), 4 * heads
        )
        span *= 2
    near = shifted(pair, "seq", 1)
    if span + 1 >= ranks:
        return near[1], maps + [alone], done + list(extras)
    far = shifted(offset, "seq", span + 1)
    joined = shifted(alone, "seq", -span)
    (incoming,) = kernel_call(carry_kernel, [shape], (far, near), 2 * heads)
    return incoming, maps + [joined], done + list(extras)


def scan_back(local, maps, ranks):
    heads = local.shape[0]
    total = local
    span = 1
    for level in range(len(maps) - 1):
        later = shifted(total, "seq", -span)
        (total,) = kernel_call(
            carry_back_kernel, [(local.shape, F32)], (later, maps[level], total), 2 * heads
        )
        span *= 2
    near = shifted(total, "seq", -1)
    if span + 1 < ranks:
        far = shifted(total, "seq", -(span + 1))
        (near,) = kernel_call(
            carry_back_kernel, [(local.shape, F32)], (far, maps[-1], near), 2 * heads
        )
    return near


def layer(
    block_input,
    mixer_gain,
    proj_weight,
    rate_weight,
    conv_weight,
    decay_log,
    decay_bias,
    write_bias,
    output_gain,
    merge_weight,
    feed_gain,
    gateup_weight,
    down_weight,
    output_grad,
):
    length, local_width = block_input.shape
    model_width, heads, width = proj_weight.shape
    dim = width // 4
    hidden_width = down_weight.shape[0]
    taps = conv_weight.shape[0]
    ranks = lax.axis_size("seq")
    sides = lax.axis_size("head")
    rank = lax.axis_index("seq")
    part = lax.axis_index("head")
    rows = length + EDGE

    edge = shifted(block_input[length - EDGE :], "seq", 1)
    gains = [jnp.broadcast_to(gain[None], (EDGE, local_width)) for gain in (mixer_gain, feed_gain)]
    (packed,) = kernel_call(
        pack_kernel,
        [((rows + 2 * EDGE + length, local_width), BF)],
        (edge, block_input, jnp.concatenate(gains, axis=0), output_grad),
        1,
    )
    whole = lax.all_gather(packed, "head", axis=1, tiled=True)
    whole, merge_sent, proj_late = lax.optimization_barrier((whole, merge_weight, proj_weight))
    inputs_ext = whole[:rows].astype(F32)
    gain_one = whole[rows].astype(F32)
    grads_full = whole[rows + 2 * EDGE :]
    merge_parts = [merge_weight]
    merge_parts += [turned(merge_sent, "head", i, sides) for i in range(1, sides)]

    scale_ext = rms_scale(inputs_ext)
    normed_ext = (inputs_ext * scale_ext * gain_one).astype(BF)
    projected = jnp.einsum("td,dhe->hte", normed_ext, proj_weight, preferred_element_type=F32)
    rates = jnp.einsum(
        "td,dhe->hte", normed_ext[EDGE:], rate_weight, preferred_element_type=F32
    )
    params = jnp.stack([decay_log, decay_bias, write_bias])

    cube = (heads, length, dim)
    square = (heads, length, length)
    pre, q, k, inverse, weights, values, scores, inner, cols, pair, alone, offset = kernel_call(
        setup_kernel,
        [
            ((heads, length, 3 * dim), F32), (cube, F32), (cube, F32), (square, F32), (cube, F32),
            (cube, F32), (square, F32), (square, F32), ((heads, length, 8), F32),
            ((2, heads, dim, dim), F32), ((heads, dim, dim), F32), ((heads, dim, dim), F32),
        ],
        (projected, rates, conv_weight, params),
        18 * heads,
        [pltpu.VMEM((rows, 3 * dim), F32)],
    )
    rate_columns = jnp.moveaxis(rate_weight, 0, 2).reshape(2 * heads, model_width).T
    wide_weight = jnp.concatenate(
        [
            proj_late.reshape(model_width, heads * width),
            jnp.pad(rate_columns, ((0, 0), (0, 128 - 2 * heads))),
        ],
        axis=1,
    )
    share = model_width // ranks
    outer, group = plane(ranks)
    places = (rank // group + jnp.arange(outer)) % outer * group + rank % group
    around = (rank // group + jnp.arange(outer)) % outer
    normed_parts = in_group(normed_ext, ranks)
    grad_parts = []
    for steps in range(outer):
        piece = lax.dynamic_slice_in_dim(
            grads_full, around[steps] * (group * share), group * share, 1
        )
        grad_parts.append(outward(piece, ranks, steps) if steps else piece)
    incoming, maps, extras = scan_states(
        pair, alone, offset, ranks,
        [(wide_weight, normed_parts, grad_parts), merge_parts],
    )
    (wide_weight, normed_parts, grad_parts), merge_parts = extras
    mixed_rows, updates, outs = kernel_call(
        outputs_kernel,
        [((length, heads * dim), BF), (cube, F32), (cube, F32)],
        (q, weights, values, scores, cols, incoming, projected, output_gain),
        3 * heads,
    )
    rows_parts = [mixed_rows] + [turned(mixed_rows, "head", i, sides) for i in range(1, sides)]
    full = (length, model_width)
    resid, feed_right, feed_sent, back, back_half, *feed_picks = kernel_call(
        functools.partial(feed_kernel, sides),
        [
            (full, F32), ((3 * hidden_width, length), BF),
            ((sides, length, local_width), BF), (full, F32), (full, BF),
        ]
        + [((length, group * share), BF)] * outer,
        [around, whole, jnp.moveaxis(gateup_weight, 0, 2), down_weight] + rows_parts + merge_parts,
        512,
        [pltpu.VMEM(full, BF)],
        scalars=1,
    )
    others = [turned(back_half, "head", i, sides) for i in range(1, sides)]
    feed_parts = {0: (feed_right, feed_picks[0])}
    for steps in range(1, outer):
        feed_parts[steps] = (
            outward(feed_right, ranks, steps), outward(feed_picks[steps], ranks, steps)
        )
    cube32 = (cube, F32)
    (
        grad_resid, grad_resid_half, grad_gain_two, douts, dupdates, dstate, dgate,
        grad_output_gain,
    ) = kernel_call(
        functools.partial(resid_back_kernel, len(others)),
        [
            (full, F32), (full, BF), ((1, model_width), F32), cube32, cube32,
            ((heads, dim, dim), F32), cube32, ((heads, dim), F32),
        ],
        [
            whole, resid, merge_weight, outs, projected, output_gain, scores, q, weights, cols,
            back, *others,
        ],
        100,
    )
    feed_out = lax.all_to_all(feed_sent, "head", 0, 0, tiled=True)
    mine_resid = lax.dynamic_slice_in_dim(resid, part * local_width, local_width, 1)
    block_output = mine_resid + jnp.sum(feed_out.astype(F32), axis=0)
    grad_gain_two = lax.dynamic_slice_in_dim(grad_gain_two, part * local_width, local_width, 1)
    half_parts = in_group(grad_resid_half, ranks)
    mixed_parts = in_group(mixed_rows, ranks)
    dq, dk, dcum = kernel_call(
        score_back_kernel,
        [(cube, F32), (cube, F32), ((heads, length, 8), F32)],
        (douts, updates, scores, q, k, cols, incoming),
        4 * heads,
    )

    def local_blocks(places, lefts, rights, which, dims, height):
        parts = [
            [picked(left[p], places, share) for left in lefts] + [right[p] for right in rights]
            for p in range(len(lefts[0]))
        ]
        return kernel_call(
            functools.partial(blocks_kernel, len(parts), len(lefts), which, dims),
            [((height, share), BF)] * places.shape[0],
            [places] + [ref for part_refs in parts for ref in part_refs],
            256,
            scalars=1,
        )

    feed_rows = 3 * hidden_width
    halfway = 2 * hidden_width
    grad_end = scan_back(dstate, maps, ranks)
    feed_blocks = local_blocks(
        (rank + jnp.arange(group)) % group,
        [[feed_parts[i][1] for i in range(outer)], grad_parts],
        [[feed_parts[i][0] for i in range(outer)]],
        ((0, (0, 0, halfway)), (1, (0, halfway, feed_rows))),
        NN,
        feed_rows,
    )
    feed_sum = inner_sum(feed_blocks, ranks)
    merge_blocks = local_blocks(places, [half_parts], [mixed_parts], ((0, (0,)),), TN, heads * dim)
    merge_blocks = [merge_blocks[0]] + [
        outward(merge_blocks[steps], ranks, steps) for steps in range(1, outer)
    ]
    span_width = heads * width + 128
    grad_rows, grad_conv, grad_params = kernel_call(
        final_back_kernel,
        [((rows, span_width), BF), ((taps, heads, 3 * dim), F32), ((heads, 128), F32)],
        (
            grad_end, dupdates, incoming, updates, inverse, inner, k, q, cols, dq, dk, dcum,
            pre, projected, conv_weight, params, dgate,
        ),
        7 * heads,
        [pltpu.VMEM((rows, 3 * dim), F32), pltpu.VMEM((rows + EDGE, 3 * dim), F32)],
    )
    right_parts = in_group(grad_rows, ranks)
    left_parts = [picked(left, places, share) for left in normed_parts]
    parts = list(zip(left_parts, right_parts))
    blocks = kernel_call(
        functools.partial(feature_major_kernel, len(parts)),
        [((share, span_width), BF)] * outer,
        [places] + [ref for part_refs in parts for ref in part_refs],
        100,
        scalars=1,
    )
    last_blocks = [blocks[0]]
    last_blocks += [outward(blocks[steps], ranks, steps) for steps in range(1, outer)]
    (sent,) = kernel_call(
        input_back_kernel,
        [((sides, rows, local_width + 128), BF)],
        (grad_rows, wide_weight, inputs_ext, gain_one[None]),
        64,
    )
    got = lax.all_to_all(sent, "head", 0, 0, tiled=True)
    got = jnp.sum(got.astype(F32), axis=0)
    mine_normed = got[:, :local_width]
    stat_total = got[:, local_width : local_width + 1] + got[:, local_width + 1 : local_width + 2]
    mine_ext = lax.dynamic_slice_in_dim(inputs_ext, part * local_width, local_width, 1)
    mine_gain = lax.dynamic_slice_in_dim(gain_one, part * local_width, local_width, 0)
    grad_gain_one = jnp.sum(mine_normed * mine_ext * scale_ext, axis=0)
    input_part = (
        scale_ext * mine_normed * mine_gain
        - mine_ext * scale_ext**3 * (stat_total / model_width)
    )
    from_next = shifted(input_part[:EDGE], "seq", -1)
    mine_resid_grad = lax.dynamic_slice_in_dim(grad_resid, part * local_width, local_width, 1)
    input_grad = mine_resid_grad + input_part[EDGE:]
    input_grad = jnp.concatenate(
        [input_grad[: length - EDGE], input_grad[length - EDGE :] + from_next], axis=0
    )

    small = [
        grad_conv.reshape(-1, 128),
        grad_output_gain.reshape(-1, 128),
        grad_params,
        grad_gain_two.reshape(-1, 128),
        grad_gain_one.reshape(-1, 128),
    ]
    ends = [0]
    for piece in small:
        ends.append(ends[-1] + piece.shape[0])
    small_parts = shared_sum(jnp.concatenate(small, axis=0), ranks)
    last_blocks, merge_blocks, small_parts, input_grad, block_output, feed_sum = (
        lax.optimization_barrier(
            (last_blocks, merge_blocks, small_parts, input_grad, block_output, feed_sum)
        )
    )
    total = ordered_sum(small_parts, rank // group)
    small = [total[start:end] for start, end in zip(ends, ends[1:])]
    conv_split = 3 * dim // ranks
    gain_split = dim // ranks
    grad_conv_mine = lax.dynamic_slice_in_dim(
        small[0].reshape(taps, heads, 3 * dim), rank * conv_split, conv_split, 2
    )
    grad_output_gain_mine = lax.dynamic_slice_in_dim(
        small[1].reshape(heads, dim), rank * gain_split, gain_split, 1
    )
    grad_params = small[2]
    grad_gain_two = small[3].reshape(-1)
    grad_gain_one = small[4].reshape(-1)
    grad_merge = sum(block.astype(F32) for block in merge_blocks)
    grad_gateup = jnp.moveaxis(feed_sum[:halfway].reshape(2, hidden_width, share), 2, 0)
    grad_down = feed_sum[halfway:]
    summed_rows = sum(block.astype(F32) for block in last_blocks)
    grad_proj_mine = summed_rows[:, : heads * width].reshape(share, heads, width)
    grad_rate_mine = summed_rows[:, heads * width : heads * (width + 2)].reshape(share, heads, 2)
    return (
        block_output,
        input_grad,
        grad_gain_one,
        grad_proj_mine,
        grad_rate_mine,
        grad_conv_mine,
        grad_params[:, 0],
        grad_params[:, 1],
        grad_params[:, 2],
        grad_output_gain_mine,
        grad_merge,
        grad_gain_two,
        grad_gateup,
        grad_down,
    )


def solution(mesh):
    return jax.shard_map(
        layer,
        mesh=mesh,
        in_specs=(
            P("seq", "head"),
            P("head"),
            P(None, "head", None),
            P(None, "head", None),
            P(None, "head", None),
            P("head"),
            P("head"),
            P("head"),
            P("head", None),
            P("head", None),
            P("head"),
            P(None, None, "head"),
            P("head", None),
            P("seq", "head"),
        ),
        out_specs=(
            P("seq", "head"),
            P("seq", "head"),
            P("head"),
            P("seq", "head", None),
            P("seq", "head", None),
            P(None, "head", "seq"),
            P("head"),
            P("head"),
            P("head"),
            P("head", "seq"),
            P("head", "seq"),
            P("head"),
            P("seq", None, "head"),
            P("head", "seq"),
        ),
        check_vma=False,
    )
```

```python
import functools

import jax
import jax.numpy as jnp
from jax import lax
from jax.experimental import pallas as pl
from jax.experimental.pallas import tpu as pltpu
from jax.sharding import PartitionSpec as P


EPSILON = 1e-06
EDGE = 8
BF = jnp.bfloat16
F32 = jnp.float32
NN = (((1,), (0,)), ((), ()))
NT = (((1,), (1,)), ((), ()))
TN = (((0,), (0,)), ((), ()))


def shifted(value, axis, steps):
    count = lax.axis_size(axis)
    pairs = [(i, i + steps) for i in range(count) if 0 <= i + steps < count]
    return lax.ppermute(value, axis, pairs)


def plane(ranks):
    inner = 1
    while inner * inner * 4 <= ranks:
        inner *= 2
    return ranks // inner, inner


def turned(value, axis, steps, group):
    count = lax.axis_size(axis)
    pairs = [(i, i // group * group + (i % group + steps) % group) for i in range(count)]
    return lax.ppermute(value, axis, pairs)


def in_group(value, ranks):
    _, inner = plane(ranks)
    return [value] + [turned(value, "seq", i, inner) for i in range(1, inner)]


def shared_sum(value, ranks):
    outer, inner = plane(ranks)
    step = 1
    while step < inner:
        other = lax.ppermute(value, "seq", [(i, i ^ step) for i in range(ranks)])
        value = value + other
        step *= 2
    return [value] + [outward(value, ranks, steps) for steps in range(1, outer)]


def ordered_sum(parts, place):
    stacked = jnp.stack(parts)
    count = len(parts)
    return sum(
        lax.dynamic_index_in_dim(stacked, (place - i) % count, 0, keepdims=False)
        for i in range(count)
    )


def outward(value, ranks, steps):
    _, inner = plane(ranks)
    pairs = [(r, (r + steps * inner) % ranks) for r in range(ranks)]
    return lax.ppermute(value, "seq", pairs)


def inner_sum(blocks, ranks):
    _, inner = plane(ranks)
    total = blocks[0].astype(F32)
    for steps in range(1, inner):
        total = total + turned(blocks[steps], "seq", steps, inner).astype(F32)
    return total


def rms_scale(rows):
    return lax.rsqrt(jnp.mean(rows * rows, axis=-1, keepdims=True) + EPSILON)


def halves(x):
    high = x.astype(BF)
    low = (x - high.astype(F32)).astype(BF)
    return high, low


def dot(a, b, dims=NN):
    ah, al = halves(a)
    bh, bl = halves(b)
    one = functools.partial(lax.dot_general, dimension_numbers=dims, preferred_element_type=F32)
    return one(ah, bh) + (one(ah, bl) + one(al, bh))


def grids(length):
    row = lax.broadcasted_iota(jnp.int32, (length, length), 0)
    col = lax.broadcasted_iota(jnp.int32, (length, length), 1)
    return row, col


def to_row(column, row, col):
    return jnp.sum(jnp.where(row == col, column, 0.0), axis=0, keepdims=True)


def to_column(line, row, col):
    return jnp.sum(jnp.where(row == col, line, 0.0), axis=1, keepdims=True)


def decay_matrix(cum, row, col):
    causal = col <= row
    gap = cum - to_row(cum, row, col)
    return jnp.where(causal, jnp.exp(jnp.where(causal, gap, 0.0)), 0.0)


def unit_lower_inverse(lower, row, col):
    length = lower.shape[0]
    identity = jnp.where(row == col, 1.0, 0.0)
    pair = (row // 2 == col // 2) & (col < row)
    inverse = identity - jnp.where(pair, lower, 0.0)
    size = 2
    while size < length:
        off = (row // (2 * size) == col // (2 * size)) & (row // size != col // size) & (col < row)
        inverse = inverse - dot(dot(inverse, jnp.where(off, lower, 0.0)), inverse)
        size *= 2
    return inverse


def pack_kernel(edge_ref, input_ref, gains_ref, grad_ref, packed_ref):
    length, _ = input_ref.shape
    rows = length + EDGE
    packed_ref[:EDGE, :] = edge_ref[...]
    packed_ref[EDGE:rows, :] = input_ref[...]
    packed_ref[rows : rows + 2 * EDGE, :] = gains_ref[...]
    packed_ref[rows + 2 * EDGE :, :] = grad_ref[...]


def setup_kernel(
    proj_ref, rates_ref, taps_ref, params_ref,
    pre_ref, q_ref, k_ref, inv_ref, w_ref, vals_ref, score_ref, inner_ref, cols_ref, map_ref, alone_ref, offset_ref,
    ext_ref,
):
    heads, rows, width = proj_ref.shape
    length = rows - EDGE
    dim = width // 4
    taps = taps_ref.shape[0]
    row, col = grids(length)
    for h in range(heads):
        ext_ref[...] = proj_ref[h, :, : 3 * dim].astype(BF).astype(F32)
        start = EDGE - taps + 1
        pre = ext_ref[start : start + length, :] * taps_ref[0, h : h + 1, :]
        for j in range(1, taps):
            pre = pre + ext_ref[start + j : start + j + length, :] * taps_ref[j, h : h + 1, :]
        pre_ref[h] = pre
        mixed = pre * jax.nn.sigmoid(pre)
        q = mixed[:, :dim]
        k = mixed[:, dim : 2 * dim]
        v = mixed[:, 2 * dim :]
        q = q * lax.rsqrt(jnp.sum(q * q, axis=1, keepdims=True) + EPSILON) * dim ** (-0.5)
        k = k * lax.rsqrt(jnp.sum(k * k, axis=1, keepdims=True) + EPSILON)
        beta = jax.nn.sigmoid(rates_ref[h, :, 0:1] + params_ref[2:3, h : h + 1])
        shift = rates_ref[h, :, 1:2] + params_ref[1:2, h : h + 1]
        soft = jnp.maximum(shift, 0.0) + jnp.log1p(jnp.exp(-jnp.abs(shift)))
        decay = -jnp.exp(params_ref[0:1, h : h + 1]) * soft
        cum = jnp.sum(jnp.where(col <= row, to_row(decay, row, col), 0.0), axis=1, keepdims=True)
        decays = decay_matrix(cum, row, col)
        growth = jnp.exp(cum)
        last = cum[length - 1 : length, :]
        remain = jnp.exp(last - cum)
        inner = jnp.where(col < row, decays * dot(k, k, NT), 0.0)
        inverse = unit_lower_inverse(beta * inner, row, col)
        weights = dot(inverse, (beta * growth) * k)
        values = dot(inverse, beta * v)
        kept = remain * k
        identity = jnp.where(row[:dim, :dim] == col[:dim, :dim], jnp.exp(last), 0.0)
        alone = identity - dot(weights, kept, TN)
        offset = dot(values, kept, TN)
        map_ref[0, h] = alone
        map_ref[1, h] = offset
        alone_ref[h] = alone.astype(BF)
        offset_ref[h] = offset
        q_ref[h] = q
        k_ref[h] = k
        inv_ref[h] = inverse
        w_ref[h] = weights
        vals_ref[h] = values
        score_ref[h] = decays * dot(q, k, NT)
        inner_ref[h] = inner
        cols_ref[h] = jnp.concatenate(
            [cum, beta, decay, jax.nn.sigmoid(shift), jnp.zeros((length, 4), F32)], axis=1
        )


def outputs_kernel(
    q_ref, w_ref, vals_ref, score_ref, cols_ref, state_ref, gate_ref, gain_ref,
    mixed_ref, upd_ref, out_ref,
):
    heads, _, dim = q_ref.shape
    for h in range(heads):
        state = state_ref[h]
        upd = vals_ref[h] - dot(w_ref[h], state, NT)
        out = jnp.exp(cols_ref[h, :, 0:1]) * dot(q_ref[h], state, NT) + dot(score_ref[h], upd)
        gate = gate_ref[h, EDGE:, 3 * dim :]
        normed = out * lax.rsqrt(jnp.mean(out * out, axis=1, keepdims=True) + EPSILON)
        normed = normed * gain_ref[h : h + 1, :] * (gate * jax.nn.sigmoid(gate))
        mixed_ref[:, h * dim : (h + 1) * dim] = normed.astype(BF)
        upd_ref[h] = upd
        out_ref[h] = out


def feed_kernel(sides, place_ref, whole_ref, gateup_ref, down_ref, *refs):
    rows_refs, merge_refs = refs[:sides], refs[sides : 2 * sides]
    resid_ref, right_ref, sent_ref, back_ref, back_half_ref, *feed_refs = refs[2 * sides :]
    feed_ref = feed_refs.pop()
    length = resid_ref.shape[0]
    rows = length + EDGE
    hidden = down_ref.shape[0]
    resid = whole_ref[EDGE:rows, :].astype(F32)
    for row_ref, merge_ref in zip(rows_refs, merge_refs):
        resid = resid + jnp.dot(row_ref[...], merge_ref[...], preferred_element_type=F32)
    resid_ref[...] = resid
    gain = whole_ref[rows + EDGE : rows + EDGE + 1, :].astype(F32)
    feed_in = (resid * rms_scale(resid) * gain).astype(BF)
    feed_ref[...] = feed_in
    for i, pick_ref in enumerate(feed_refs):
        size = pick_ref.shape[1] // 2
        pick_ref[:, :size] = columns_of(feed_ref, place_ref, i, size)
        columns = pl.ds(pl.multiple_of(place_ref[i] * size, size), size)
        pick_ref[:, size:] = whole_ref[rows + 2 * EDGE :, columns]
    one = functools.partial(lax.dot_general, preferred_element_type=F32)
    gate = one(gateup_ref[0], feed_in, NT)
    up = one(gateup_ref[1], feed_in, NT)
    grad_hidden = one(down_ref[...], whole_ref[rows + 2 * EDGE :, :], NT)
    sigma = jax.nn.sigmoid(gate)
    active = (gate * sigma * up).astype(BF)
    grad_gate = (grad_hidden * up * sigma * (1.0 + gate * (1.0 - sigma))).astype(BF)
    grad_up = (grad_hidden * gate * sigma).astype(BF)
    right_ref[:hidden, :] = grad_gate
    right_ref[hidden : 2 * hidden, :] = grad_up
    right_ref[2 * hidden :, :] = active
    back = one(grad_gate, gateup_ref[0], TN) + one(grad_up, gateup_ref[1], TN)
    back_ref[...] = back
    back_half_ref[...] = back.astype(BF)
    out = one(active, down_ref[...], TN).astype(BF)
    local = out.shape[1] // sides
    for side in range(sides):
        sent_ref[side] = out[:, side * local : (side + 1) * local]


def resid_back_kernel(
    others, whole_ref, resid_ref, merge_ref, out_ref, gate_ref, gain_ref, score_ref, q_ref, w_ref,
    cols_ref, back_ref, *refs,
):
    (
        grad_ref, half_ref, dfeed_ref, dout_ref, dupd_ref, dstate_ref, dgate_ref, dgain_ref, sent_ref,
    ) = refs[others:]
    heads, length, dim = q_ref.shape
    rows = length + EDGE
    back = back_ref[...]
    for other_ref in refs[:others]:
        back = back + other_ref[...].astype(F32)
    resid = resid_ref[...]
    scale = rms_scale(resid)
    dfeed_ref[...] = jnp.sum(back * resid * scale, axis=0, keepdims=True)
    weighted = back * whole_ref[rows + EDGE : rows + EDGE + 1, :].astype(F32)
    grad = whole_ref[rows + 2 * EDGE :, :].astype(F32) + scale * weighted
    grad = grad - resid * (scale * scale * scale) * jnp.mean(
        weighted * resid, axis=1, keepdims=True
    )
    grad_ref[...] = grad
    half = grad.astype(BF)
    half_ref[...] = half
    grad_mixed = lax.dot_general(half, merge_ref[...], NT, preferred_element_type=F32)
    for h in range(heads):
        grad = grad_mixed[:, h * dim : (h + 1) * dim]
        out = out_ref[h]
        scale = lax.rsqrt(jnp.mean(out * out, axis=1, keepdims=True) + EPSILON)
        normed = out * scale
        gate = gate_ref[h, EDGE:, 3 * dim :]
        sigma = jax.nn.sigmoid(gate)
        gain = gain_ref[h : h + 1, :]
        silu = gate * sigma
        dgain_ref[h : h + 1, :] = jnp.sum(grad * normed * silu, axis=0, keepdims=True)
        dgate_ref[h] = grad * normed * gain * (sigma * (1.0 + gate * (1.0 - sigma)))
        inside = grad * gain * silu
        dout = scale * (inside - normed * jnp.mean(inside * normed, axis=1, keepdims=True))
        dupd = dot(score_ref[h], dout, TN)
        grown = jnp.exp(cols_ref[h, :, 0:1]) * dout
        dstate = dot(grown, q_ref[h], TN) - dot(dupd, w_ref[h], TN)
        dstate_ref[h] = dstate
        sent_ref[h] = dstate.astype(BF)
        dout_ref[h] = dout
        dupd_ref[h] = dupd


def score_back_kernel(
    dout_ref, upd_ref, score_ref, q_ref, k_ref, cols_ref, state_ref,
    dq_ref, dk_ref, dcum_ref,
):
    heads, length, _ = q_ref.shape
    row, col = grids(length)
    for h in range(heads):
        dout = dout_ref[h]
        q = q_ref[h]
        cum = cols_ref[h, :, 0:1]
        dscore = jnp.where(col <= row, dot(dout, upd_ref[h], NT), 0.0)
        dinner = dscore * decay_matrix(cum, row, col)
        grown = dot(jnp.exp(cum) * dout, state_ref[h])
        dq_ref[h] = grown + dot(dinner, k_ref[h])
        dk_ref[h] = dot(dinner, q, TN)
        both = dscore * score_ref[h]
        dcum = jnp.sum(both, axis=1, keepdims=True) + jnp.sum(q * grown, axis=1, keepdims=True)
        dcum = dcum - to_column(jnp.sum(both, axis=0, keepdims=True), row, col)
        dcum_ref[h] = jnp.broadcast_to(dcum, (length, 8))


def final_back_kernel(
    dend_ref, dupd_ref, state_ref, upd_ref, inv_ref, inner_ref, k_ref, q_ref, cols_ref,
    dq_ref, dk_ref, dcum_ref, pre_ref, proj_ref, taps_ref, params_ref, dgate_ref,
    rows_ref, dtaps_ref, dparams_ref,
    ext_ref, pad_ref,
):
    heads, length, dim = q_ref.shape
    taps = taps_ref.shape[0]
    rows = length + EDGE
    row, col = grids(length)
    width = 4 * dim
    pad_ref[...] = jnp.zeros_like(pad_ref)
    rows_ref[:, heads * width :] = jnp.zeros((rows, rows_ref.shape[1] - heads * width), BF)
    lane = lax.broadcasted_iota(jnp.int32, (1, 128), 1)
    for h in range(heads):
        dend = dend_ref[h]
        state = state_ref[h]
        upd = upd_ref[h]
        k = k_ref[h]
        inner = inner_ref[h]
        cum = cols_ref[h, :, 0:1]
        beta = cols_ref[h, :, 1:2]
        decay = cols_ref[h, :, 2:3]
        soft_slope = cols_ref[h, :, 3:4]
        growth = jnp.exp(cum)
        last = cum[length - 1 : length, :]
        remain = jnp.exp(last - cum)
        kept = remain * k
        pre = pre_ref[h]
        sigma = jax.nn.sigmoid(pre)
        mixed = pre * sigma
        v = mixed[:, 2 * dim :]
        dupd = dupd_ref[h] + dot(kept, dend, NT)
        solved = dot(inv_ref[h], dupd, TN)
        dkept = dot(upd, dend)
        dright = -dot(solved, state)
        dlower = jnp.where(col < row, -dot(solved, upd, NT), 0.0)
        across = jnp.sum(dright * k, axis=1, keepdims=True)
        dlow_inner = dlower * inner
        dbeta_inner = jnp.sum(dlow_inner, axis=1, keepdims=True)
        dbeta = dbeta_inner + growth * across + jnp.sum(solved * v, axis=1, keepdims=True)
        both = beta * dlow_inner
        dinner = (dlower * beta) * decay_matrix(cum, row, col)
        dk = dk_ref[h] + dot(dinner, k) + dot(dinner, k, TN)
        dk = dk + (beta * growth) * dright + remain * dkept
        tail = jnp.sum(dkept * kept, axis=1, keepdims=True)
        dcum = dcum_ref[h, :, 0:1] + beta * dbeta_inner
        dcum = dcum - to_column(jnp.sum(both, axis=0, keepdims=True), row, col)
        dcum = dcum + (beta * growth) * across - tail
        dlast = jnp.sum(tail, axis=0, keepdims=True)
        held = jnp.sum(jnp.sum(state * dend, axis=1, keepdims=True), axis=0, keepdims=True)
        dlast = dlast + jnp.exp(last) * held
        ddecay = jnp.sum(jnp.where(col >= row, to_row(dcum, row, col), 0.0), axis=1, keepdims=True)
        ddecay = ddecay + dlast
        dv = beta * solved
        dshift = ddecay * (-jnp.exp(params_ref[0:1, h : h + 1])) * soft_slope
        dwrite = dbeta * beta * (1.0 - beta)
        total_log = jnp.sum(ddecay * decay, axis=0, keepdims=True)
        total_bias = jnp.sum(dshift, axis=0, keepdims=True)
        total_write = jnp.sum(dwrite, axis=0, keepdims=True)
        line = jnp.where(lane == 0, total_log, 0.0) + jnp.where(lane == 1, total_bias, 0.0)
        dparams_ref[h : h + 1, :] = line + jnp.where(lane == 2, total_write, 0.0)
        place = heads * width
        rate_lanes = jnp.where(lane == 2 * h, dwrite, 0.0) + jnp.where(lane == 2 * h + 1, dshift, 0.0)
        rows_ref[EDGE:, place : place + 128] += rate_lanes.astype(BF)
        q_raw = mixed[:, :dim]
        k_raw = mixed[:, dim : 2 * dim]
        q_scale = lax.rsqrt(jnp.sum(q_raw * q_raw, axis=1, keepdims=True) + EPSILON)
        k_scale = lax.rsqrt(jnp.sum(k_raw * k_raw, axis=1, keepdims=True) + EPSILON)
        q_unit = q_raw * q_scale
        dq = dq_ref[h] * dim ** (-0.5)
        dq = q_scale * (dq - q_unit * jnp.sum(dq * q_unit, axis=1, keepdims=True))
        dk = k_scale * (dk - k * jnp.sum(dk * k, axis=1, keepdims=True))
        slope = sigma * (1.0 + pre * (1.0 - sigma))
        dpre = jnp.concatenate([dq, dk, dv], axis=1) * slope
        pad_ref[EDGE : EDGE + length, :] = dpre
        ext_ref[...] = proj_ref[h, :, : 3 * dim].astype(BF).astype(F32)
        start = EDGE - taps + 1
        total = jnp.zeros((rows, 3 * dim), F32)
        for j in range(taps):
            dtaps_ref[j, h : h + 1, :] = jnp.sum(
                dpre * ext_ref[start + j : start + j + length, :], axis=0, keepdims=True
            )
            total = total + pad_ref[taps - 1 - j : taps - 1 - j + rows, :] * taps_ref[j, h : h + 1, :]
        rows_ref[:, h * width : h * width + 3 * dim] = total.astype(BF)
        rows_ref[:EDGE, h * width + 3 * dim : (h + 1) * width] = jnp.zeros((EDGE, dim), BF)
        rows_ref[EDGE:, h * width + 3 * dim : (h + 1) * width] = dgate_ref[h].astype(BF)


def picked(left, places, share, base=0):
    if share % 128 == 0:
        return left
    starts = [base + places[z] * share for z in range(places.shape[0])]
    return jnp.stack([lax.dynamic_slice_in_dim(left, start, share, 1) for start in starts])


def columns_of(left_ref, place_ref, z, share, base=0):
    if len(left_ref.shape) == 3:
        return left_ref[z]
    return left_ref[:, pl.ds(pl.multiple_of(base + place_ref[z] * share, share), share)]


def blocks_kernel(parts, bases, which, dims, place_ref, *refs):
    outer = place_ref.shape[0]
    lefts = len(bases)
    rights = (len(refs) - outer) // parts - lefts
    for z in range(outer):
        out_ref = refs[len(refs) - outer + z]
        share = out_ref.shape[1]
        at = 0
        for a, b in which:
            total = None
            for p in range(parts):
                left = columns_of(
                    refs[p * (lefts + rights) + a], place_ref, z, share, bases[a]
                )
                right_ref = refs[p * (lefts + rights) + lefts + b[0]]
                right = right_ref[b[1] : b[2], :] if len(b) > 1 else right_ref[...]
                one = lax.dot_general(right, left, dims, preferred_element_type=F32)
                total = one if total is None else total + one
            out_ref[at : at + total.shape[0], :] = total.astype(BF)
            at += total.shape[0]


def feature_major_kernel(parts, place_ref, *refs):
    for z in range(place_ref.shape[0]):
        out_ref = refs[2 * parts + z]
        share = out_ref.shape[0]
        total = None
        for p in range(parts):
            left = columns_of(refs[2 * p], place_ref, z, share)
            one = lax.dot_general(left, refs[2 * p + 1][...], TN, preferred_element_type=F32)
            total = one if total is None else total + one
        out_ref[...] = total.astype(BF)


def input_back_kernel(rows_ref, weight_ref, inputs_ref, gain_ref, sent_ref):
    sides, rows, wide = sent_ref.shape
    local = wide - 128
    grad = lax.dot_general(rows_ref[...], weight_ref[...], NT, preferred_element_type=F32)
    stat = jnp.sum(grad * gain_ref[...] * inputs_ref[...], axis=1, keepdims=True)
    high, low = halves(stat)
    lane = lax.broadcasted_iota(jnp.int32, (rows, 128), 1)
    stats = jnp.where(lane == 0, high.astype(F32), 0.0) + jnp.where(lane == 1, low.astype(F32), 0.0)
    for side in range(sides):
        sent_ref[side, :, :local] = grad[:, side * local : (side + 1) * local].astype(BF)
        sent_ref[side, :, local:] = stats.astype(BF)


def compose_kernel(early_ref, late_ref, both_ref, alone_ref, offset_ref):
    for h in range(early_ref.shape[1]):
        later = late_ref[0, h]
        alone = dot(early_ref[0, h], later)
        offset = dot(early_ref[1, h], later) + late_ref[1, h]
        both_ref[0, h] = alone
        both_ref[1, h] = offset
        alone_ref[h] = alone.astype(BF)
        offset_ref[h] = offset


def carry_kernel(first_ref, pair_ref, sum_ref):
    for h in range(first_ref.shape[0]):
        sum_ref[h] = dot(first_ref[h], pair_ref[0, h]) + pair_ref[1, h]


def carry_back_kernel(first_ref, map_ref, second_ref, sum_ref, sent_ref):
    for h in range(first_ref.shape[0]):
        one = lax.dot_general(first_ref[h], map_ref[h], NT, preferred_element_type=F32)
        total = one + second_ref[h].astype(F32)
        sum_ref[h] = total
        sent_ref[h] = total.astype(BF)


def kernel_call(body, outs, args, dots, scratch=(), scalars=0):
    vmem = pl.BlockSpec(memory_space=pltpu.VMEM)
    smem = pl.BlockSpec(memory_space=pltpu.SMEM)
    shapes = [jax.ShapeDtypeStruct(shape, kind) for shape, kind in outs]
    total = sum(a.size * a.dtype.itemsize for a in args)
    return pl.pallas_call(
        body,
        out_shape=shapes,
        in_specs=[smem] * scalars + [vmem] * (len(args) - scalars),
        out_specs=[vmem] * len(outs),
        scratch_shapes=list(scratch),
        cost_estimate=pl.CostEstimate(
            flops=dots * 6 * 128**3, bytes_accessed=total, transcendentals=0
        ),
    )(*args)


def scan_states(pair, alone, offset, ranks, extras):
    heads = pair.shape[1]
    shape = (pair.shape[1:], F32)
    half = (pair.shape[1:], BF)
    maps = []
    done = []
    span = 1
    while 2 * span < ranks:
        early = shifted(pair, "seq", span)
        joined = shifted(alone, "seq", 1 - span) if span > 1 else alone
        if extras:
            early, ready = lax.optimization_barrier((early, extras[0]))
            extras = extras[1:]
            done.append(ready)
        maps.append(joined)
        pair, alone, offset = kernel_call(
            compose_kernel, [(pair.shape, F32), half, shape], (early, pair), 4 * heads
        )
        span *= 2
    near = shifted(pair, "seq", 1)
    if span + 1 >= ranks:
        return near[1], maps + [alone], done + list(extras)
    far = shifted(offset, "seq", span + 1)
    joined = shifted(alone, "seq", -span)
    (incoming,) = kernel_call(carry_kernel, [shape], (far, near), 2 * heads)
    return incoming, maps + [joined], done + list(extras)


def scan_back(total, sent, maps, ranks):
    heads = total.shape[0]
    kinds = [(total.shape, F32), (total.shape, BF)]
    span = 1
    for level in range(len(maps) - 1):
        later = shifted(sent, "seq", -span)
        total, sent = kernel_call(
            carry_back_kernel, kinds, (later, maps[level], total), 2 * heads
        )
        span *= 2
    near = shifted(sent, "seq", -1)
    if span + 1 < ranks:
        far = shifted(sent, "seq", -(span + 1))
        near, _ = kernel_call(carry_back_kernel, kinds, (far, maps[-1], near), 2 * heads)
    return near.astype(F32)


def layer(
    block_input,
    mixer_gain,
    proj_weight,
    rate_weight,
    conv_weight,
    decay_log,
    decay_bias,
    write_bias,
    output_gain,
    merge_weight,
    feed_gain,
    gateup_weight,
    down_weight,
    output_grad,
):
    length, local_width = block_input.shape
    model_width, heads, width = proj_weight.shape
    dim = width // 4
    hidden_width = down_weight.shape[0]
    taps = conv_weight.shape[0]
    ranks = lax.axis_size("seq")
    sides = lax.axis_size("head")
    rank = lax.axis_index("seq")
    part = lax.axis_index("head")
    rows = length + EDGE

    edge = shifted(block_input[length - EDGE :], "seq", 1)
    gains = [jnp.broadcast_to(gain[None], (EDGE, local_width)) for gain in (mixer_gain, feed_gain)]
    (packed,) = kernel_call(
        pack_kernel,
        [((rows + 2 * EDGE + length, local_width), BF)],
        (edge, block_input, jnp.concatenate(gains, axis=0), output_grad),
        1,
    )
    whole = lax.all_gather(packed, "head", axis=1, tiled=True)
    whole, merge_sent, proj_late = lax.optimization_barrier((whole, merge_weight, proj_weight))
    inputs_ext = whole[:rows].astype(F32)
    gain_one = whole[rows].astype(F32)
    merge_parts = [merge_weight]
    merge_parts += [turned(merge_sent, "head", i, sides) for i in range(1, sides)]

    scale_ext = rms_scale(inputs_ext)
    normed_ext = (inputs_ext * scale_ext * gain_one).astype(BF)
    projected = jnp.einsum("td,dhe->hte", normed_ext, proj_weight, preferred_element_type=F32)
    rates = jnp.einsum(
        "td,dhe->hte", normed_ext[EDGE:], rate_weight, preferred_element_type=F32
    )
    params = jnp.stack([decay_log, decay_bias, write_bias])

    cube = (heads, length, dim)
    square = (heads, length, length)
    pre, q, k, inverse, weights, values, scores, inner, cols, pair, alone, offset = kernel_call(
        setup_kernel,
        [
            ((heads, length, 3 * dim), F32), (cube, F32), (cube, F32), (square, F32), (cube, F32),
            (cube, F32), (square, F32), (square, F32), ((heads, length, 8), F32),
            ((2, heads, dim, dim), F32), ((heads, dim, dim), BF), ((heads, dim, dim), F32),
        ],
        (projected, rates, conv_weight, params),
        18 * heads,
        [pltpu.VMEM((rows, 3 * dim), F32)],
    )
    rate_columns = jnp.moveaxis(rate_weight, 0, 2).reshape(2 * heads, model_width).T
    wide_weight = jnp.concatenate(
        [
            proj_late.reshape(model_width, heads * width),
            jnp.pad(rate_columns, ((0, 0), (0, 128 - 2 * heads))),
        ],
        axis=1,
    )
    share = model_width // ranks
    outer, group = plane(ranks)
    places = (rank // group + jnp.arange(outer)) % outer * group + rank % group
    around = (rank // group + jnp.arange(outer)) % outer
    normed_parts = in_group(normed_ext, ranks)
    incoming, maps, (wide_weight, merge_parts) = scan_states(
        pair, alone, offset, ranks, [wide_weight, merge_parts]
    )
    mixed_rows, updates, outs = kernel_call(
        outputs_kernel,
        [((length, heads * dim), BF), (cube, F32), (cube, F32)],
        (q, weights, values, scores, cols, incoming, projected, output_gain),
        3 * heads,
    )
    rows_parts = [mixed_rows] + [turned(mixed_rows, "head", i, sides) for i in range(1, sides)]
    full = (length, model_width)
    resid, feed_right, feed_sent, back, back_half, *feed_picks = kernel_call(
        functools.partial(feed_kernel, sides),
        [
            (full, F32), ((3 * hidden_width, length), BF),
            ((sides, length, local_width), BF), (full, F32), (full, BF),
        ]
        + [((length, 2 * group * share), BF)] * outer,
        [around, whole, jnp.moveaxis(gateup_weight, 0, 2), down_weight] + rows_parts + merge_parts,
        512,
        [pltpu.VMEM(full, BF)],
        scalars=1,
    )
    others = [turned(back_half, "head", i, sides) for i in range(1, sides)]
    right_parts, left_parts = [feed_right], [feed_picks[0]]
    for i in range(1, outer):
        right_parts.append(outward(feed_right, ranks, i))
        left_parts.append(outward(feed_picks[i], ranks, i))
    cube32 = (cube, F32)
    (
        grad_resid, grad_resid_half, grad_gain_two, douts, dupdates, dstate, dgate,
        grad_output_gain, dstate_sent,
    ) = kernel_call(
        functools.partial(resid_back_kernel, len(others)),
        [
            (full, F32), (full, BF), ((1, model_width), F32), cube32, cube32,
            ((heads, dim, dim), F32), cube32, ((heads, dim), F32), ((heads, dim, dim), BF),
        ],
        [
            whole, resid, merge_weight, outs, projected, output_gain, scores, q, weights, cols,
            back, *others,
        ],
        100,
    )
    feed_out = lax.all_to_all(feed_sent, "head", 0, 0, tiled=True)
    mine_resid = lax.dynamic_slice_in_dim(resid, part * local_width, local_width, 1)
    block_output = mine_resid + jnp.sum(feed_out.astype(F32), axis=0)
    grad_gain_two = lax.dynamic_slice_in_dim(grad_gain_two, part * local_width, local_width, 1)
    half_parts = in_group(grad_resid_half, ranks)
    mixed_parts = in_group(mixed_rows, ranks)
    dq, dk, dcum = kernel_call(
        score_back_kernel,
        [(cube, F32), (cube, F32), ((heads, length, 8), F32)],
        (douts, updates, scores, q, k, cols, incoming),
        4 * heads,
    )

    def local_blocks(places, lefts, bases, rights, which, dims, height):
        parts = [
            [picked(left[p], places, share, base) for left, base in zip(lefts, bases)]
            + [right[p] for right in rights]
            for p in range(len(lefts[0]))
        ]
        return kernel_call(
            functools.partial(blocks_kernel, len(parts), bases, which, dims),
            [((height, share), BF)] * places.shape[0],
            [places] + [ref for part_refs in parts for ref in part_refs],
            256,
            scalars=1,
        )

    feed_rows = 3 * hidden_width
    halfway = 2 * hidden_width
    grad_end = scan_back(dstate, dstate_sent, maps, ranks)
    feed_blocks = local_blocks(
        (rank + jnp.arange(group)) % group,
        [left_parts, left_parts],
        (0, group * share),
        [right_parts],
        ((0, (0, 0, halfway)), (1, (0, halfway, feed_rows))),
        NN,
        feed_rows,
    )
    feed_sum = inner_sum(feed_blocks, ranks)
    merge_blocks = local_blocks(
        places, [half_parts], (0,), [mixed_parts], ((0, (0,)),), TN, heads * dim
    )
    merge_blocks = [merge_blocks[0]] + [
        outward(merge_blocks[steps], ranks, steps) for steps in range(1, outer)
    ]
    span_width = heads * width + 128
    grad_rows, grad_conv, grad_params = kernel_call(
        final_back_kernel,
        [((rows, span_width), BF), ((taps, heads, 3 * dim), F32), ((heads, 128), F32)],
        (
            grad_end, dupdates, incoming, updates, inverse, inner, k, q, cols, dq, dk, dcum,
            pre, projected, conv_weight, params, dgate,
        ),
        7 * heads,
        [pltpu.VMEM((rows, 3 * dim), F32), pltpu.VMEM((rows + EDGE, 3 * dim), F32)],
    )
    row_parts = in_group(grad_rows, ranks)
    parts = list(zip([picked(left, places, share) for left in normed_parts], row_parts))
    blocks = kernel_call(
        functools.partial(feature_major_kernel, len(parts)),
        [((share, span_width), BF)] * outer,
        [places] + [ref for part_refs in parts for ref in part_refs],
        100,
        scalars=1,
    )
    last_blocks = [blocks[0]]
    last_blocks += [outward(blocks[steps], ranks, steps) for steps in range(1, outer)]
    (sent,) = kernel_call(
        input_back_kernel,
        [((sides, rows, local_width + 128), BF)],
        (grad_rows, wide_weight, inputs_ext, gain_one[None]),
        64,
    )
    got = lax.all_to_all(sent, "head", 0, 0, tiled=True)
    got = jnp.sum(got.astype(F32), axis=0)
    mine_normed = got[:, :local_width]
    stat_total = got[:, local_width : local_width + 1] + got[:, local_width + 1 : local_width + 2]
    mine_ext = lax.dynamic_slice_in_dim(inputs_ext, part * local_width, local_width, 1)
    mine_gain = lax.dynamic_slice_in_dim(gain_one, part * local_width, local_width, 0)
    grad_gain_one = jnp.sum(mine_normed * mine_ext * scale_ext, axis=0)
    input_part = (
        scale_ext * mine_normed * mine_gain
        - mine_ext * scale_ext**3 * (stat_total / model_width)
    )
    from_next = shifted(input_part[:EDGE], "seq", -1)
    mine_resid_grad = lax.dynamic_slice_in_dim(grad_resid, part * local_width, local_width, 1)
    input_grad = mine_resid_grad + input_part[EDGE:]
    input_grad = jnp.concatenate(
        [input_grad[: length - EDGE], input_grad[length - EDGE :] + from_next], axis=0
    )

    small = [
        grad_conv.reshape(-1, 128),
        grad_output_gain.reshape(-1, 128),
        grad_params,
        grad_gain_two.reshape(-1, 128),
        grad_gain_one.reshape(-1, 128),
    ]
    ends = [0]
    for piece in small:
        ends.append(ends[-1] + piece.shape[0])
    small_parts = shared_sum(jnp.concatenate(small, axis=0), ranks)
    last_blocks, merge_blocks, small_parts, input_grad, block_output, feed_sum = (
        lax.optimization_barrier(
            (last_blocks, merge_blocks, small_parts, input_grad, block_output, feed_sum)
        )
    )
    total = ordered_sum(small_parts, rank // group)
    small = [total[start:end] for start, end in zip(ends, ends[1:])]
    conv_split = 3 * dim // ranks
    gain_split = dim // ranks
    grad_conv_mine = lax.dynamic_slice_in_dim(
        small[0].reshape(taps, heads, 3 * dim), rank * conv_split, conv_split, 2
    )
    grad_output_gain_mine = lax.dynamic_slice_in_dim(
        small[1].reshape(heads, dim), rank * gain_split, gain_split, 1
    )
    grad_params = small[2]
    grad_gain_two = small[3].reshape(-1)
    grad_gain_one = small[4].reshape(-1)
    grad_merge = sum(block.astype(F32) for block in merge_blocks)
    grad_gateup = jnp.moveaxis(feed_sum[:halfway].reshape(2, hidden_width, share), 2, 0)
    grad_down = feed_sum[halfway:]
    summed_rows = sum(block.astype(F32) for block in last_blocks)
    grad_proj_mine = summed_rows[:, : heads * width].reshape(share, heads, width)
    grad_rate_mine = summed_rows[:, heads * width : heads * (width + 2)].reshape(share, heads, 2)
    return (
        block_output,
        input_grad,
        grad_gain_one,
        grad_proj_mine,
        grad_rate_mine,
        grad_conv_mine,
        grad_params[:, 0],
        grad_params[:, 1],
        grad_params[:, 2],
        grad_output_gain_mine,
        grad_merge,
        grad_gain_two,
        grad_gateup,
        grad_down,
    )


def solution(mesh):
    return jax.shard_map(
        layer,
        mesh=mesh,
        in_specs=(
            P("seq", "head"),
            P("head"),
            P(None, "head", None),
            P(None, "head", None),
            P(None, "head", None),
            P("head"),
            P("head"),
            P("head"),
            P("head", None),
            P("head", None),
            P("head"),
            P(None, None, "head"),
            P("head", None),
            P("seq", "head"),
        ),
        out_specs=(
            P("seq", "head"),
            P("seq", "head"),
            P("head"),
            P("seq", "head", None),
            P("seq", "head", None),
            P(None, "head", "seq"),
            P("head"),
            P("head"),
            P("head"),
            P("head", "seq"),
            P("head", "seq"),
            P("head"),
            P("seq", None, "head"),
            P("head", "seq"),
        ),
        check_vma=False,
    )
```
